256 devices in a mesh: dp: 32 (over y, z), tensor: 8 (over x, core).
Axes of the slice: x: 4, y: 4, z: 8, core: 2. Of those that a mesh axis runs over, the one named last changes fastest.
Arguments:
- tokens: bfloat16 [4096, 3072], P('dp', 'tensor'), may hold values from -6 to 6
- grad_out: bfloat16 [4096, 3072], P('dp', 'tensor'), may hold values from -6 to 6
- expert_ids: int32 [4096, 2], P('dp'), may hold values from 0 to 7, as said below
- gate_probs: float32 [4096, 2], P('dp'), may hold values from 0.2 to 1
- w_gate: bfloat16 [32, 3072, 2048], P('dp', None, 'tensor'), may hold values from -0.109375 to 0.109375
- w_up: bfloat16 [32, 3072, 2048], P('dp', None, 'tensor'), may hold values from -0.109375 to 0.109375
- w_down: bfloat16 [32, 2048, 3072], P('dp', 'tensor'), may hold values from -0.0625 to 0.0625
Outputs:
- input_grad: bfloat16 [4096, 3072], P('dp', 'tensor')
- grad_gate: bfloat16 [32, 3072, 2048], P('dp', None, 'tensor')
- grad_up: bfloat16 [32, 3072, 2048], P('dp', None, 'tensor')
- grad_down: bfloat16 [32, 2048, 3072], P('dp', 'tensor')
The draws below stay inside these ranges and needn't reach their ends.
Inputs may be any that keep to these rules, and one draw needn't show every extreme that they name: `expert_ids`: A token's two experts differ. Among the 128 tokens of one index of dp (aligned blocks of rows), no expert is named more than 33 times, and one expert, the same in every block, is named exactly 33 times in each block.
All inputs are finite; a program needn't handle non-finite values.
Results may differ from the reference program's by a relative error of at most 0.015.
Values may be sent and summed in bfloat16 or wider, within the bound.
A program may use at most 128 MiB of HBM per device.

```python
import jax
import jax.numpy as jnp
from jax import lax

D = 3072
FF = 8192
EXPERTS = 8
TOP = 2
TOK_DEV = 128
CAP = 33
TOKENS = 4096
SLICES = 4
FF_DEV = 256
N_DP = 32
N_TENSOR = 8


def route_block(key, hot_expert):
    key_perm, key_jitter, key_order, key_swap = jax.random.split(key, 4)
    others = jax.random.permutation(key_perm, EXPERTS - 1).astype(jnp.int32)
    others = jnp.where(others >= hot_expert, others + 1, others)
    spare_slots = 2 * TOK_DEV - CAP
    base_count = spare_slots // (EXPERTS - 1)
    extra_count = spare_slots % (EXPERTS - 1)
    jitter = CAP - base_count - 1
    halves = (EXPERTS - 1) // 2
    shifts = jax.random.randint(key_jitter, (halves,), 0, jitter + 1).astype(jnp.int32)
    changes = jnp.concatenate([shifts, -shifts, jnp.zeros((EXPERTS - 1 - 2 * halves,), jnp.int32)])
    counts = base_count + (jnp.arange(EXPERTS - 1) < extra_count).astype(jnp.int32) + changes
    sizes_all = jnp.concatenate([jnp.full((1,), CAP, jnp.int32), counts.astype(jnp.int32)])
    group_order = jnp.concatenate([jnp.reshape(hot_expert, (1,)), others])
    bounds = jnp.cumsum(sizes_all)
    places = jnp.arange(2 * TOK_DEV, dtype=jnp.int32)
    group_index = jnp.sum((places[:, None] >= bounds[None, :]).astype(jnp.int32), axis=1)
    chosen = group_order[group_index]
    first_pick = chosen[:TOK_DEV]
    second_pick = chosen[TOK_DEV:]
    swap_flags = jax.random.randint(key_swap, (TOK_DEV,), 0, 2)
    pairing = jnp.where(swap_flags[:, None] == 1, jnp.stack([second_pick, first_pick], axis=1), jnp.stack([first_pick, second_pick], axis=1))
    token_order = jax.random.permutation(key_order, TOK_DEV)
    return pairing[token_order]


def draw_expert_ids(key, part):
    key_hot, key_blocks = jax.random.split(jax.random.fold_in(key, 17), 2)
    hot_expert = jax.random.randint(key_hot, (), 0, EXPERTS).astype(jnp.int32)
    block_keys = jax.random.split(key_blocks, TOKENS // TOK_DEV)
    blocks = jax.vmap(route_block, in_axes=(0, None))(block_keys, hot_expert)
    return blocks.reshape(TOKENS, TOP).astype(jnp.int32)


def steps_of(stream_key, dims, shards, low, top_value):
    loudness = 1.0
    for dim, shards_of in shards:
        steps = jax.random.uniform(jax.random.fold_in(jax.random.fold_in(stream_key, 6), dim), (shards_of,), jnp.float32, low / len(shards), top_value / len(shards))
        loudness = loudness * jnp.repeat(jnp.exp(steps), dims[dim] // shards_of).reshape((-1,) + (1,) * (len(dims) - 1 - dim))
    return loudness


def normal_values(stream_key, shape, width, reach, cuts=(), kind=jnp.bfloat16):
    factor_of = steps_of(stream_key, shape, cuts, -0.22, 0.18) if cuts else 1.0
    array = jax.random.normal(stream_key, shape, jnp.float32) * width * factor_of
    return jnp.minimum(jnp.maximum(array, -reach), reach).astype(kind)


def setup_inputs(seed: int = 0) -> dict:
    arg_keys = jax.random.split(jax.random.key(seed), 8)
    return {
        "tokens": normal_values(arg_keys[0], (TOKENS, D), 1.0, 6.0, ((0, 32), (1, 8))),
        "grad_out": normal_values(arg_keys[1], (TOKENS, D), 1.0, 6.0, ((0, 32), (1, 8))),
        "expert_ids": draw_expert_ids(jax.random.fold_in(arg_keys[7], 71), 0),
        "gate_probs": jnp.clip(0.2 + 0.8 * jax.random.uniform(arg_keys[3], (TOKENS, TOP), jnp.float32) ** steps_of(arg_keys[3], (TOKENS, TOP), ((0, 32),), -0.2, 0.2), 0.2, 1.0),
        "w_gate": normal_values(arg_keys[4], (EXPERTS * SLICES, D, FF // SLICES), D ** -0.5, 0.109375, ((0, 32), (2, 8))),
        "w_up": normal_values(arg_keys[5], (EXPERTS * SLICES, D, FF // SLICES), D ** -0.5, 0.109375, ((0, 32), (2, 8))),
        "w_down": normal_values(arg_keys[6], (EXPERTS * SLICES, FF // SLICES, D), FF ** -0.5, 0.0625, ((0, 32), (1, 8))),
    }


def block_sum(gate_grad, up_grad, gate_full, up_full):
    def add_block(block, running):
        start = block * FF_DEV
        gate_piece = lax.dynamic_slice_in_dim(gate_grad, start, FF_DEV, 1)
        up_piece = lax.dynamic_slice_in_dim(up_grad, start, FF_DEV, 1)
        gate_rows = lax.dynamic_slice_in_dim(gate_full, start, FF_DEV, 1)
        up_rows = lax.dynamic_slice_in_dim(up_full, start, FF_DEV, 1)
        part = jnp.dot(gate_piece, gate_rows.T, preferred_element_type=jnp.float32)
        part = part + jnp.dot(up_piece, up_rows.T, preferred_element_type=jnp.float32)
        rounded = lax.optimization_barrier(part.astype(jnp.bfloat16))
        return running + rounded.astype(jnp.float32)

    start_value = jnp.zeros((gate_grad.shape[0], D), jnp.float32)
    return lax.fori_loop(0, SLICES * N_TENSOR, add_block, start_value)


def reference(tokens, grad_out, expert_ids, gate_probs, w_gate, w_up, w_down):
    pair_count = TOKENS * TOP
    flat_ids = expert_ids.reshape(-1).astype(jnp.int32)
    experts_row = jnp.arange(EXPERTS, dtype=jnp.int32)
    onehot = (flat_ids[:, None] == experts_row[None, :]).astype(jnp.int32)
    rank_index = jnp.sum((jnp.cumsum(onehot, axis=0) - onehot) * onehot, axis=1).astype(jnp.int32)
    rows_most = N_DP * CAP
    lookup = jnp.full((EXPERTS, rows_most), pair_count, jnp.int32)
    lookup = lookup.at[flat_ids, rank_index].set(jnp.arange(pair_count, dtype=jnp.int32))
    token_rows = jnp.concatenate([tokens, jnp.zeros((1, D), jnp.bfloat16)], axis=0)
    scaled = (gate_probs[:, :, None] * grad_out[:, None, :].astype(jnp.float32)).astype(jnp.bfloat16)
    scaled = jnp.concatenate([scaled.reshape(pair_count, D), jnp.zeros((1, D), jnp.bfloat16)], axis=0)
    input_total = jnp.zeros((TOKENS + 1, D), jnp.float32)
    gate_list = []
    up_list = []
    down_list = []
    for expert in range(EXPERTS):
        chosen = lookup[expert]
        token_index = jnp.where(chosen < pair_count, chosen // TOP, TOKENS).astype(jnp.int32)
        expert_rows = token_rows[token_index]
        expert_grads = scaled[chosen]
        first_row = expert * SLICES
        gate_full = jnp.transpose(w_gate[first_row:first_row + SLICES], (1, 0, 2)).reshape(D, FF)
        up_full = jnp.transpose(w_up[first_row:first_row + SLICES], (1, 0, 2)).reshape(D, FF)
        down_full = w_down[first_row:first_row + SLICES].reshape(FF, D)
        gate_value = jnp.dot(expert_rows, gate_full, preferred_element_type=jnp.float32)
        up_value = jnp.dot(expert_rows, up_full, preferred_element_type=jnp.float32)
        sigmoid_value = jax.nn.sigmoid(gate_value)
        silu_value = gate_value * sigmoid_value
        hidden = (silu_value * up_value).astype(jnp.bfloat16)
        hidden_grad = jnp.dot(expert_grads, down_full.T, preferred_element_type=jnp.float32)
        gate_grad = (hidden_grad * up_value * sigmoid_value * (1.0 + gate_value * (1.0 - sigmoid_value))).astype(jnp.bfloat16)
        up_grad = (hidden_grad * silu_value).astype(jnp.bfloat16)
        row_grads = block_sum(gate_grad, up_grad, gate_full, up_full)
        input_total = input_total.at[token_index].add(row_grads)
        gate_total = jnp.dot(expert_rows.T, gate_grad, preferred_element_type=jnp.float32)
        up_total = jnp.dot(expert_rows.T, up_grad, preferred_element_type=jnp.float32)
        down_total = jnp.dot(hidden.T, expert_grads, preferred_element_type=jnp.float32)
        gate_list.append(jnp.transpose(gate_total.reshape(D, SLICES, FF // SLICES), (1, 0, 2)).astype(jnp.bfloat16))
        up_list.append(jnp.transpose(up_total.reshape(D, SLICES, FF // SLICES), (1, 0, 2)).astype(jnp.bfloat16))
        down_list.append(down_total.reshape(SLICES, FF // SLICES, D).astype(jnp.bfloat16))
    input_grad = input_total[:TOKENS].astype(jnp.bfloat16)
    grad_gate = jnp.concatenate(gate_list, axis=0)
    grad_up = jnp.concatenate(up_list, axis=0)
    grad_down = jnp.concatenate(down_list, axis=0)
    return (input_grad, grad_gate, grad_up, grad_down)
```

```python
import jax
import jax.numpy as jnp
from jax import lax
from jax.sharding import PartitionSpec as P

EXPERTS = 8
TOP = 2
CAP = 33


def expert_work(rows, grads, gate_shard, up_shard, down_shard):
    f32 = jnp.float32
    gate_value = jnp.einsum("trf,tfh->rh", rows, gate_shard, preferred_element_type=f32)
    up_value = jnp.einsum("trf,tfh->rh", rows, up_shard, preferred_element_type=f32)
    sigmoid_value = jax.nn.sigmoid(gate_value)
    silu_value = gate_value * sigmoid_value
    hidden = (silu_value * up_value).astype(jnp.bfloat16)
    hidden_grad = jnp.einsum("trf,htf->rh", grads, down_shard, preferred_element_type=f32)
    gate_grad = (
        hidden_grad * up_value * sigmoid_value * (1.0 + gate_value * (1.0 - sigmoid_value))
    ).astype(jnp.bfloat16)
    up_grad = (hidden_grad * silu_value).astype(jnp.bfloat16)
    row_part = (
        jnp.einsum("rh,tfh->trf", gate_grad, gate_shard, preferred_element_type=f32)
        + jnp.einsum("rh,tfh->trf", up_grad, up_shard, preferred_element_type=f32)
    ).astype(jnp.bfloat16)
    gate_total = jnp.einsum("trf,rh->tfh", rows, gate_grad, preferred_element_type=f32)
    up_total = jnp.einsum("trf,rh->tfh", rows, up_grad, preferred_element_type=f32)
    down_total = jnp.einsum("rh,trf->htf", hidden, grads, preferred_element_type=f32)
    return (
        row_part,
        gate_total.astype(jnp.bfloat16),
        up_total.astype(jnp.bfloat16),
        down_total.astype(jnp.bfloat16),
    )


def shards(tokens, grad_out, expert_ids, gate_probs, w_gate, w_up, w_down):
    dp_size = lax.axis_size("dp")
    tp_size = lax.axis_size("tensor")
    slices = dp_size // EXPERTS
    token_count = tokens.shape[0]
    feat = tokens.shape[1]
    pair_count = token_count * TOP
    flat_ids = expert_ids.reshape(-1)
    experts_row = jnp.arange(EXPERTS, dtype=jnp.int32)
    onehot = (flat_ids[:, None] == experts_row[None, :]).astype(jnp.int32)
    slot_index = jnp.sum((jnp.cumsum(onehot, axis=0) - onehot) * onehot, axis=1)
    positions = jnp.arange(CAP, dtype=jnp.int32)
    matches = (flat_ids[None, None, :] == experts_row[:, None, None]) & (
        slot_index[None, None, :] == positions[None, :, None]
    )
    assignment = jnp.arange(pair_count, dtype=jnp.int32)
    lookup = jnp.sum(jnp.where(matches, assignment[None, None, :], 0), axis=2)
    lookup = lookup + jnp.where(jnp.any(matches, axis=2), 0, pair_count)
    owners = jnp.arange(dp_size, dtype=jnp.int32) // slices
    send_pairs = lookup[owners]
    send_tokens = jnp.where(send_pairs < pair_count, send_pairs // TOP, token_count)
    slice_row = jnp.arange(slices, dtype=jnp.int32)
    back_index = (flat_ids[:, None] * slices + slice_row[None, :]) * CAP + slot_index[:, None]

    def padded(rows_in):
        return jnp.concatenate([rows_in, jnp.zeros((1, rows_in.shape[1]), rows_in.dtype)], axis=0)

    sent_rows = padded(tokens)[send_tokens]
    product = gate_probs[:, :, None] * grad_out[:, None, :].astype(jnp.float32)
    sent_grads = padded(product.astype(jnp.bfloat16).reshape(pair_count, feat))[send_pairs]
    sent = jnp.stack([sent_rows, sent_grads], axis=0)
    got = lax.all_to_all(sent, "dp", split_axis=1, concat_axis=1, tiled=True)
    whole = lax.all_gather(got, "tensor", axis=0, tiled=False)
    rows_count = dp_size * CAP
    got_rows = whole[:, 0].reshape(tp_size, rows_count, feat)
    got_grads = whole[:, 1].reshape(tp_size, rows_count, feat)
    hid = w_gate.shape[2]
    gate_shard = w_gate[0].reshape(tp_size, feat, hid)
    up_shard = w_up[0].reshape(tp_size, feat, hid)
    down_shard = w_down[0].reshape(hid, tp_size, feat)
    row_part, gate_total, up_total, down_total = expert_work(
        got_rows, got_grads, gate_shard, up_shard, down_shard
    )
    reduced = lax.psum_scatter(row_part, "tensor", scatter_dimension=0, tiled=True)
    returned = lax.all_to_all(
        reduced.reshape(dp_size, CAP, feat), "dp", split_axis=0, concat_axis=0, tiled=True
    )
    flat_back = returned.reshape(rows_count, feat)
    picked = flat_back[back_index].reshape(token_count, TOP * slices, feat)
    input_grad = jnp.sum(picked, axis=1, dtype=jnp.float32).astype(jnp.bfloat16)
    return (
        input_grad,
        gate_total.reshape(1, tp_size * feat, hid),
        up_total.reshape(1, tp_size * feat, hid),
        down_total.reshape(1, hid, tp_size * feat),
    )


def solution(mesh):
    placed = (
        P("dp", "tensor"),
        P("dp", "tensor"),
        P("dp", None),
        P("dp", None),
        P("dp", None, "tensor"),
        P("dp", None, "tensor"),
        P("dp", "tensor", None),
    )
    return jax.shard_map(
        shards,
        mesh=mesh,
        in_specs=placed,
        out_specs=(
            P("dp", "tensor"),
            P("dp", None, "tensor"),
            P("dp", None, "tensor"),
            P("dp", "tensor", None),
        ),
        check_vma=False,
    )
```

```python
import jax
import jax.numpy as jnp
from jax import lax
from jax.sharding import PartitionSpec as P

EXPERTS = 8
TOP = 2
CAP = 33


def expert_work(rows, grads, gate_shard, up_shard, down_shard):
    f32 = jnp.float32
    gate_value = jnp.einsum("trf,tfh->rh", rows, gate_shard, preferred_element_type=f32)
    up_value = jnp.einsum("trf,tfh->rh", rows, up_shard, preferred_element_type=f32)
    sigmoid_value = jax.nn.sigmoid(gate_value)
    silu_value = gate_value * sigmoid_value
    hidden = (silu_value * up_value).astype(jnp.bfloat16)
    hidden_grad = jnp.einsum("trf,htf->rh", grads, down_shard, preferred_element_type=f32)
    gate_grad = (
        hidden_grad * up_value * sigmoid_value * (1.0 + gate_value * (1.0 - sigmoid_value))
    ).astype(jnp.bfloat16)
    up_grad = (hidden_grad * silu_value).astype(jnp.bfloat16)
    row_part = (
        jnp.einsum("rh,tfh->trf", gate_grad, gate_shard, preferred_element_type=f32)
        + jnp.einsum("rh,tfh->trf", up_grad, up_shard, preferred_element_type=f32)
    ).astype(jnp.bfloat16)
    gate_total = jnp.einsum("trf,rh->tfh", rows, gate_grad, preferred_element_type=f32)
    up_total = jnp.einsum("trf,rh->tfh", rows, up_grad, preferred_element_type=f32)
    down_total = jnp.einsum("rh,trf->htf", hidden, grads, preferred_element_type=f32)
    return (
        row_part,
        gate_total.astype(jnp.bfloat16),
        up_total.astype(jnp.bfloat16),
        down_total.astype(jnp.bfloat16),
    )


def shards(tokens, grad_out, expert_ids, gate_probs, w_gate, w_up, w_down):
    dp_size = lax.axis_size("dp")
    tp_size = lax.axis_size("tensor")
    slices = dp_size // EXPERTS
    token_count = tokens.shape[0]
    feat = tokens.shape[1]
    pair_count = token_count * TOP
    flat_ids = expert_ids.reshape(-1)
    experts_row = jnp.arange(EXPERTS, dtype=jnp.int32)
    onehot = (flat_ids[:, None] == experts_row[None, :]).astype(jnp.int32)
    slot_index = jnp.sum((jnp.cumsum(onehot, axis=0) - onehot) * onehot, axis=1)
    positions = jnp.arange(CAP, dtype=jnp.int32)
    matches = (flat_ids[None, None, :] == experts_row[:, None, None]) & (
        slot_index[None, None, :] == positions[None, :, None]
    )
    assignment = jnp.arange(pair_count, dtype=jnp.int32)
    lookup = jnp.sum(jnp.where(matches, assignment[None, None, :], 0), axis=2)
    lookup = lookup + jnp.where(jnp.any(matches, axis=2), 0, pair_count)
    owners = jnp.arange(dp_size, dtype=jnp.int32) // slices
    send_pairs = lookup[owners]
    send_tokens = jnp.where(send_pairs < pair_count, send_pairs // TOP, token_count)
    slice_row = jnp.arange(slices, dtype=jnp.int32)
    back_index = (flat_ids[:, None] * slices + slice_row[None, :]) * CAP + slot_index[:, None]

    bf16 = jnp.bfloat16
    f32 = jnp.float32
    flat_tokens = send_tokens.reshape(-1)
    flat_pairs = send_pairs.reshape(-1)
    pick_tokens = (flat_tokens[:, None] == jnp.arange(token_count)[None, :]).astype(bf16)
    pick_pairs = (flat_pairs[:, None] == assignment[None, :]).astype(bf16)
    scaled = (gate_probs[:, :, None] * grad_out[:, None, :].astype(f32)).astype(bf16)
    sent_rows = jnp.dot(pick_tokens, tokens, preferred_element_type=f32).astype(bf16)
    sent_grads = jnp.dot(pick_pairs, scaled.reshape(pair_count, feat), preferred_element_type=f32)
    sent_grads = sent_grads.astype(bf16)
    rows_count = dp_size * CAP
    got_rows = lax.all_to_all(
        sent_rows.reshape(dp_size, CAP, feat), "dp", split_axis=0, concat_axis=0, tiled=True
    )
    whole_rows = lax.all_gather(got_rows.reshape(rows_count, feat), "tensor", axis=0, tiled=True)
    got_grads = lax.all_to_all(
        sent_grads.reshape(dp_size, CAP, feat), "dp", split_axis=0, concat_axis=0, tiled=True
    )
    whole_grads = lax.all_gather(
        got_grads.reshape(rows_count, feat), "tensor", axis=0, tiled=True
    )
    got_rows = whole_rows.reshape(tp_size, rows_count, feat)
    got_grads = whole_grads.reshape(tp_size, rows_count, feat)
    hid = w_gate.shape[2]
    gate_shard = w_gate[0].reshape(tp_size, feat, hid)
    up_shard = w_up[0].reshape(tp_size, feat, hid)
    down_shard = w_down[0].reshape(hid, tp_size, feat)
    row_part, gate_total, up_total, down_total = expert_work(
        got_rows, got_grads, gate_shard, up_shard, down_shard
    )
    reduced = lax.psum_scatter(row_part, "tensor", scatter_dimension=0, tiled=True)
    reduced, gate_total, up_total, down_total = lax.optimization_barrier(
        (reduced, gate_total, up_total, down_total)
    )
    returned = lax.all_to_all(
        reduced.reshape(dp_size, CAP, feat), "dp", split_axis=0, concat_axis=0, tiled=True
    )
    flat_back = returned.reshape(rows_count, feat)
    back_flat = back_index.reshape(token_count, TOP * slices)
    rows_iota = jnp.arange(rows_count, dtype=jnp.int32)
    gather_back = jnp.sum(
        (back_flat[:, :, None] == rows_iota[None, None, :]).astype(f32), axis=1
    ).astype(bf16)
    input_grad = jnp.dot(gather_back, flat_back, preferred_element_type=f32).astype(bf16)
    return (
        input_grad,
        gate_total.reshape(1, tp_size * feat, hid),
        up_total.reshape(1, tp_size * feat, hid),
        down_total.reshape(1, hid, tp_size * feat),
    )


def solution(mesh):
    placed = (
        P("dp", "tensor"),
        P("dp", "tensor"),
        P("dp", None),
        P("dp", None),
        P("dp", None, "tensor"),
        P("dp", None, "tensor"),
        P("dp", "tensor", None),
    )
    return jax.shard_map(
        shards,
        mesh=mesh,
        in_specs=placed,
        out_specs=(
            P("dp", "tensor"),
            P("dp", None, "tensor"),
            P("dp", None, "tensor"),
            P("dp", "tensor", None),
        ),
        check_vma=False,
    )
```

```python
import functools

import jax
import jax.numpy as jnp
from jax import lax
from jax.experimental import pallas as pl
from jax.experimental.pallas import tpu as pltpu
from jax.sharding import PartitionSpec as P

EXPERTS = 8
TOP = 2
CAP = 33
MESH = pl.DeviceIdType.MESH


def a2a_kernel(n, x_ref, y_ref, send_sem, recv_sem, local_sem):
    me = lax.axis_index("dp")
    tp = lax.axis_index("tensor")
    barrier = pltpu.get_barrier_semaphore()

    def peer(i):
        return lax.rem(me + 1 + i, n)

    def greet(i, carry):
        pl.semaphore_signal(barrier, inc=1, device_id=(peer(i), tp), device_id_type=MESH)
        return carry

    lax.fori_loop(0, n - 1, greet, 0)
    pl.semaphore_wait(barrier, n - 1)
    local = pltpu.make_async_copy(x_ref.at[me], y_ref.at[me], local_sem)
    local.start()

    def outgoing(p):
        return pltpu.make_async_remote_copy(
            src_ref=x_ref.at[p], dst_ref=y_ref.at[me], send_sem=send_sem.at[p],
            recv_sem=recv_sem.at[me], device_id=(p, tp), device_id_type=MESH)

    def incoming(p):
        return pltpu.make_async_remote_copy(
            src_ref=x_ref.at[me], dst_ref=y_ref.at[p], send_sem=send_sem.at[p],
            recv_sem=recv_sem.at[p], device_id=(p, tp), device_id_type=MESH)

    def start(i, carry):
        outgoing(peer(i)).start()
        return carry

    lax.fori_loop(0, n - 1, start, 0)

    def finish(i, carry):
        p = peer(i)
        outgoing(p).wait_send()
        incoming(p).wait_recv()
        return carry

    lax.fori_loop(0, n - 1, finish, 0)
    local.wait()


def dp_all_to_all(x, n, cid):
    return pl.pallas_call(
        functools.partial(a2a_kernel, n),
        out_shape=jax.ShapeDtypeStruct(x.shape, x.dtype),
        in_specs=[pl.BlockSpec(memory_space=pl.ANY)],
        out_specs=pl.BlockSpec(memory_space=pl.ANY),
        scratch_shapes=[
            pltpu.SemaphoreType.DMA((n,)),
            pltpu.SemaphoreType.DMA((n,)),
            pltpu.SemaphoreType.DMA,
        ],
        compiler_params=pltpu.CompilerParams(collective_id=cid, has_side_effects=True),
    )(x)


def expert_work(rows, grads, gate_shard, up_shard, down_shard):
    f32 = jnp.float32
    gate_value = jnp.einsum("trf,tfh->rh", rows, gate_shard, preferred_element_type=f32)
    up_value = jnp.einsum("trf,tfh->rh", rows, up_shard, preferred_element_type=f32)
    sigmoid_value = jax.nn.sigmoid(gate_value)
    silu_value = gate_value * sigmoid_value
    hidden = (silu_value * up_value).astype(jnp.bfloat16)
    hidden_grad = jnp.einsum("trf,htf->rh", grads, down_shard, preferred_element_type=f32)
    gate_grad = (
        hidden_grad * up_value * sigmoid_value * (1.0 + gate_value * (1.0 - sigmoid_value))
    ).astype(jnp.bfloat16)
    up_grad = (hidden_grad * silu_value).astype(jnp.bfloat16)
    row_part = (
        jnp.einsum("rh,tfh->trf", gate_grad, gate_shard, preferred_element_type=f32)
        + jnp.einsum("rh,tfh->trf", up_grad, up_shard, preferred_element_type=f32)
    ).astype(jnp.bfloat16)
    gate_total = jnp.einsum("trf,rh->tfh", rows, gate_grad, preferred_element_type=f32)
    up_total = jnp.einsum("trf,rh->tfh", rows, up_grad, preferred_element_type=f32)
    down_total = jnp.einsum("rh,trf->htf", hidden, grads, preferred_element_type=f32)
    return (
        row_part,
        gate_total.astype(jnp.bfloat16),
        up_total.astype(jnp.bfloat16),
        down_total.astype(jnp.bfloat16),
    )


def shards(tokens, grad_out, expert_ids, gate_probs, w_gate, w_up, w_down):
    dp_size = lax.axis_size("dp")
    tp_size = lax.axis_size("tensor")
    slices = dp_size // EXPERTS
    token_count = tokens.shape[0]
    feat = tokens.shape[1]
    pair_count = token_count * TOP
    flat_ids = expert_ids.reshape(-1)
    experts_row = jnp.arange(EXPERTS, dtype=jnp.int32)
    onehot = (flat_ids[:, None] == experts_row[None, :]).astype(jnp.int32)
    slot_index = jnp.sum((jnp.cumsum(onehot, axis=0) - onehot) * onehot, axis=1)
    positions = jnp.arange(CAP, dtype=jnp.int32)
    matches = (flat_ids[None, None, :] == experts_row[:, None, None]) & (
        slot_index[None, None, :] == positions[None, :, None]
    )
    assignment = jnp.arange(pair_count, dtype=jnp.int32)
    lookup = jnp.sum(jnp.where(matches, assignment[None, None, :], 0), axis=2)
    lookup = lookup + jnp.where(jnp.any(matches, axis=2), 0, pair_count)
    owners = jnp.arange(dp_size, dtype=jnp.int32) // slices
    send_pairs = lookup[owners]
    send_tokens = jnp.where(send_pairs < pair_count, send_pairs // TOP, token_count)
    slice_row = jnp.arange(slices, dtype=jnp.int32)
    back_index = (flat_ids[:, None] * slices + slice_row[None, :]) * CAP + slot_index[:, None]

    bf16 = jnp.bfloat16
    f32 = jnp.float32
    flat_tokens = send_tokens.reshape(-1)
    flat_pairs = send_pairs.reshape(-1)
    pick_tokens = (flat_tokens[:, None] == jnp.arange(token_count)[None, :]).astype(bf16)
    pick_pairs = (flat_pairs[:, None] == assignment[None, :]).astype(bf16)
    scaled = (gate_probs[:, :, None] * grad_out[:, None, :].astype(f32)).astype(bf16)
    sent_rows = jnp.dot(pick_tokens, tokens, preferred_element_type=f32).astype(bf16)
    sent_grads = jnp.dot(pick_pairs, scaled.reshape(pair_count, feat), preferred_element_type=f32)
    sent_grads = sent_grads.astype(bf16)
    rows_count = dp_size * CAP
    got_rows = dp_all_to_all(sent_rows.reshape(dp_size, CAP, feat), dp_size, 0)
    whole_rows = lax.all_gather(got_rows.reshape(rows_count, feat), "tensor", axis=0, tiled=True)
    got_grads = dp_all_to_all(sent_grads.reshape(dp_size, CAP, feat), dp_size, 1)
    whole_grads = lax.all_gather(
        got_grads.reshape(rows_count, feat), "tensor", axis=0, tiled=True
    )
    got_rows = whole_rows.reshape(tp_size, rows_count, feat)
    got_grads = whole_grads.reshape(tp_size, rows_count, feat)
    hid = w_gate.shape[2]
    gate_shard = w_gate[0].reshape(tp_size, feat, hid)
    up_shard = w_up[0].reshape(tp_size, feat, hid)
    down_shard = w_down[0].reshape(hid, tp_size, feat)
    row_part, gate_total, up_total, down_total = expert_work(
        got_rows, got_grads, gate_shard, up_shard, down_shard
    )
    reduced = lax.psum_scatter(row_part, "tensor", scatter_dimension=0, tiled=True)
    reduced, gate_total, up_total, down_total = lax.optimization_barrier(
        (reduced, gate_total, up_total, down_total)
    )
    returned = dp_all_to_all(reduced.reshape(dp_size, CAP, feat), dp_size, 2)
    flat_back = returned.reshape(rows_count, feat)
    back_flat = back_index.reshape(token_count, TOP * slices)
    rows_iota = jnp.arange(rows_count, dtype=jnp.int32)
    gather_back = jnp.sum(
        (back_flat[:, :, None] == rows_iota[None, None, :]).astype(f32), axis=1
    ).astype(bf16)
    input_grad = jnp.dot(gather_back, flat_back, preferred_element_type=f32).astype(bf16)
    return (
        input_grad,
        gate_total.reshape(1, tp_size * feat, hid),
        up_total.reshape(1, tp_size * feat, hid),
        down_total.reshape(1, hid, tp_size * feat),
    )


def solution(mesh):
    placed = (
        P("dp", "tensor"),
        P("dp", "tensor"),
        P("dp", None),
        P("dp", None),
        P("dp", None, "tensor"),
        P("dp", None, "tensor"),
        P("dp", "tensor", None),
    )
    return jax.shard_map(
        shards,
        mesh=mesh,
        in_specs=placed,
        out_specs=(
            P("dp", "tensor"),
            P("dp", None, "tensor"),
            P("dp", None, "tensor"),
            P("dp", "tensor", None),
        ),
        check_vma=False,
    )
```

```python
import functools

import jax
import jax.numpy as jnp
from jax import lax
from jax.experimental import pallas as pl
from jax.experimental.pallas import tpu as pltpu
from jax.sharding import PartitionSpec as P

EXPERTS = 8
TOP = 2
CAP = 33
MESH = pl.DeviceIdType.MESH


def a2a_kernel(n, x_ref, y_ref, send_sem, recv_sem, local_sem):
    me = lax.axis_index("dp")
    tx = lax.axis_index("tx")
    tc = lax.axis_index("tc")
    barrier = pltpu.get_barrier_semaphore()

    def peer(i):
        return lax.rem(me + 1 + i, n)

    def greet(i, carry):
        pl.semaphore_signal(barrier, inc=1, device_id=(peer(i), tx, tc), device_id_type=MESH)
        return carry

    lax.fori_loop(0, n - 1, greet, 0)
    pl.semaphore_wait(barrier, n - 1)
    local = pltpu.make_async_copy(x_ref.at[me], y_ref.at[me], local_sem)
    local.start()

    def outgoing(p):
        return pltpu.make_async_remote_copy(
            src_ref=x_ref.at[p], dst_ref=y_ref.at[me], send_sem=send_sem.at[p],
            recv_sem=recv_sem.at[me], device_id=(p, tx, tc), device_id_type=MESH)

    def incoming(p):
        return pltpu.make_async_remote_copy(
            src_ref=x_ref.at[me], dst_ref=y_ref.at[p], send_sem=send_sem.at[p],
            recv_sem=recv_sem.at[p], device_id=(p, tx, tc), device_id_type=MESH)

    def start(i, carry):
        outgoing(peer(i)).start()
        return carry

    lax.fori_loop(0, n - 1, start, 0)

    def finish(i, carry):
        p = peer(i)
        outgoing(p).wait_send()
        incoming(p).wait_recv()
        return carry

    lax.fori_loop(0, n - 1, finish, 0)
    local.wait()


def dp_all_to_all(x, n, cid):
    return pl.pallas_call(
        functools.partial(a2a_kernel, n),
        out_shape=jax.ShapeDtypeStruct(x.shape, x.dtype),
        in_specs=[pl.BlockSpec(memory_space=pl.ANY)],
        out_specs=pl.BlockSpec(memory_space=pl.ANY),
        scratch_shapes=[
            pltpu.SemaphoreType.DMA((n,)),
            pltpu.SemaphoreType.DMA((n,)),
            pltpu.SemaphoreType.DMA,
        ],
        compiler_params=pltpu.CompilerParams(collective_id=cid, has_side_effects=True),
    )(x)


def expert_work(rows, grads, gate_shard, up_shard, down_shard):
    f32 = jnp.float32
    gate_value = jnp.einsum("cxrf,xcfh->rh", rows, gate_shard, preferred_element_type=f32)
    up_value = jnp.einsum("cxrf,xcfh->rh", rows, up_shard, preferred_element_type=f32)
    sigmoid_value = jax.nn.sigmoid(gate_value)
    silu_value = gate_value * sigmoid_value
    hidden = (silu_value * up_value).astype(jnp.bfloat16)
    hidden_grad = jnp.einsum("cxrf,hxcf->rh", grads, down_shard, preferred_element_type=f32)
    gate_grad = (
        hidden_grad * up_value * sigmoid_value * (1.0 + gate_value * (1.0 - sigmoid_value))
    ).astype(jnp.bfloat16)
    up_grad = (hidden_grad * silu_value).astype(jnp.bfloat16)
    row_part = (
        jnp.einsum("rh,xcfh->cxrf", gate_grad, gate_shard, preferred_element_type=f32)
        + jnp.einsum("rh,xcfh->cxrf", up_grad, up_shard, preferred_element_type=f32)
    ).astype(jnp.bfloat16)
    gate_total = jnp.einsum("cxrf,rh->xcfh", rows, gate_grad, preferred_element_type=f32)
    up_total = jnp.einsum("cxrf,rh->xcfh", rows, up_grad, preferred_element_type=f32)
    down_total = jnp.einsum("rh,cxrf->hxcf", hidden, grads, preferred_element_type=f32)
    return (
        row_part,
        gate_total.astype(jnp.bfloat16),
        up_total.astype(jnp.bfloat16),
        down_total.astype(jnp.bfloat16),
    )


def shards(tokens, grad_out, expert_ids, gate_probs, w_gate, w_up, w_down):
    dp_size = lax.axis_size("dp")
    slices = dp_size // EXPERTS
    token_count = tokens.shape[0]
    feat = tokens.shape[1]
    pair_count = token_count * TOP
    flat_ids = expert_ids.reshape(-1)
    experts_row = jnp.arange(EXPERTS, dtype=jnp.int32)
    onehot = (flat_ids[:, None] == experts_row[None, :]).astype(jnp.int32)
    slot_index = jnp.sum((jnp.cumsum(onehot, axis=0) - onehot) * onehot, axis=1)
    positions = jnp.arange(CAP, dtype=jnp.int32)
    matches = (flat_ids[None, None, :] == experts_row[:, None, None]) & (
        slot_index[None, None, :] == positions[None, :, None]
    )
    assignment = jnp.arange(pair_count, dtype=jnp.int32)
    lookup = jnp.sum(jnp.where(matches, assignment[None, None, :], 0), axis=2)
    lookup = lookup + jnp.where(jnp.any(matches, axis=2), 0, pair_count)
    owners = jnp.arange(dp_size, dtype=jnp.int32) // slices
    send_pairs = lookup[owners]
    send_tokens = jnp.where(send_pairs < pair_count, send_pairs // TOP, token_count)
    slice_row = jnp.arange(slices, dtype=jnp.int32)
    back_index = (flat_ids[:, None] * slices + slice_row[None, :]) * CAP + slot_index[:, None]

    bf16 = jnp.bfloat16
    f32 = jnp.float32
    flat_tokens = send_tokens.reshape(-1)
    flat_pairs = send_pairs.reshape(-1)
    pick_tokens = (flat_tokens[:, None] == jnp.arange(token_count)[None, :]).astype(bf16)
    pick_pairs = (flat_pairs[:, None] == assignment[None, :]).astype(bf16)
    scaled = (gate_probs[:, :, None] * grad_out[:, None, :].astype(f32)).astype(bf16)
    sent_rows = jnp.dot(pick_tokens, tokens, preferred_element_type=f32).astype(bf16)
    sent_grads = jnp.dot(pick_pairs, scaled.reshape(pair_count, feat), preferred_element_type=f32)
    sent_grads = sent_grads.astype(bf16)
    rows_count = dp_size * CAP
    got_rows = dp_all_to_all(sent_rows.reshape(dp_size, CAP, feat), dp_size, 0)
    x_size = lax.axis_size("tx")
    c_size = lax.axis_size("tc")

    def gather_features(got):
        along_x = lax.all_gather(got.reshape(rows_count, feat), "tx", axis=0, tiled=True)
        both = lax.all_gather(along_x, "tc", axis=0, tiled=True)
        return both.reshape(c_size, x_size, rows_count, feat)

    got_rows = gather_features(got_rows)
    got_grads = dp_all_to_all(sent_grads.reshape(dp_size, CAP, feat), dp_size, 1)
    got_grads = gather_features(got_grads)
    hid = w_gate.shape[2]
    gate_shard = w_gate[0].reshape(x_size, c_size, feat, hid)
    up_shard = w_up[0].reshape(x_size, c_size, feat, hid)
    down_shard = w_down[0].reshape(hid, x_size, c_size, feat)
    row_part, gate_total, up_total, down_total = expert_work(
        got_rows, got_grads, gate_shard, up_shard, down_shard
    )
    core = lax.axis_index("tc")
    mine = lax.dynamic_index_in_dim(row_part, core, axis=0, keepdims=True)
    theirs = lax.dynamic_index_in_dim(row_part, 1 - core, axis=0, keepdims=True)
    arrived = lax.ppermute(theirs, "tc", perm=[(0, 1), (1, 0)])
    on_chip = (mine.astype(f32) + arrived.astype(f32)).astype(jnp.bfloat16)
    reduced = lax.psum_scatter(on_chip, "tx", scatter_dimension=1, tiled=True)
    reduced, gate_total, up_total, down_total = lax.optimization_barrier(
        (reduced, gate_total, up_total, down_total)
    )
    returned = dp_all_to_all(reduced.reshape(dp_size, CAP, feat), dp_size, 2)
    flat_back = returned.reshape(rows_count, feat)
    back_flat = back_index.reshape(token_count, TOP * slices)
    rows_iota = jnp.arange(rows_count, dtype=jnp.int32)
    gather_back = jnp.sum(
        (back_flat[:, :, None] == rows_iota[None, None, :]).astype(f32), axis=1
    ).astype(bf16)
    input_grad = jnp.dot(gather_back, flat_back, preferred_element_type=f32).astype(bf16)
    return (
        input_grad,
        gate_total.reshape(1, x_size * c_size * feat, hid),
        up_total.reshape(1, x_size * c_size * feat, hid),
        down_total.reshape(1, hid, x_size * c_size * feat),
    )


def solution(mesh):
    chip_x = mesh.shape["tensor"] // 2
    mesh = jax.sharding.Mesh(
        mesh.devices.reshape(mesh.shape["dp"], chip_x, 2), ("dp", "tx", "tc")
    )
    tensor = ("tx", "tc")
    placed = (
        P("dp", tensor),
        P("dp", tensor),
        P("dp", None),
        P("dp", None),
        P("dp", None, tensor),
        P("dp", None, tensor),
        P("dp", tensor, None),
    )
    return jax.shard_map(
        shards,
        mesh=mesh,
        in_specs=placed,
        out_specs=(
            P("dp", tensor),
            P("dp", None, tensor),
            P("dp", None, tensor),
            P("dp", tensor, None),
        ),
        check_vma=False,
    )
```

```python
import functools

import jax
import jax.numpy as jnp
from jax import lax
from jax.experimental import pallas as pl
from jax.experimental.pallas import tpu as pltpu
from jax.sharding import PartitionSpec as P

EXPERTS = 8
TOP = 2
CAP = 33
MESH = pl.DeviceIdType.MESH


def a2a_kernel(n, x_ref, y_ref, send_sem, recv_sem, local_sem):
    me = lax.axis_index("dp")
    tp = lax.axis_index("tensor")
    barrier = pltpu.get_barrier_semaphore()

    def peer(i):
        return lax.rem(me + 1 + i, n)

    def greet(i, carry):
        pl.semaphore_signal(barrier, inc=1, device_id=(peer(i), tp), device_id_type=MESH)
        return carry

    lax.fori_loop(0, n - 1, greet, 0)
    pl.semaphore_wait(barrier, n - 1)
    local = pltpu.make_async_copy(x_ref.at[me], y_ref.at[me], local_sem)
    local.start()

    def outgoing(p):
        return pltpu.make_async_remote_copy(
            src_ref=x_ref.at[p], dst_ref=y_ref.at[me], send_sem=send_sem.at[p],
            recv_sem=recv_sem.at[me], device_id=(p, tp), device_id_type=MESH)

    def incoming(p):
        return pltpu.make_async_remote_copy(
            src_ref=x_ref.at[me], dst_ref=y_ref.at[p], send_sem=send_sem.at[p],
            recv_sem=recv_sem.at[p], device_id=(p, tp), device_id_type=MESH)

    def start(i, carry):
        outgoing(peer(i)).start()
        return carry

    lax.fori_loop(0, n - 1, start, 0)

    def finish(i, carry):
        p = peer(i)
        outgoing(p).wait_send()
        incoming(p).wait_recv()
        return carry

    lax.fori_loop(0, n - 1, finish, 0)
    local.wait()


def dp_all_to_all(x, n, cid):
    return pl.pallas_call(
        functools.partial(a2a_kernel, n),
        out_shape=jax.ShapeDtypeStruct(x.shape, x.dtype),
        in_specs=[pl.BlockSpec(memory_space=pl.ANY)],
        out_specs=pl.BlockSpec(memory_space=pl.ANY),
        scratch_shapes=[
            pltpu.SemaphoreType.DMA((n,)),
            pltpu.SemaphoreType.DMA((n,)),
            pltpu.SemaphoreType.DMA,
        ],
        compiler_params=pltpu.CompilerParams(collective_id=cid, has_side_effects=True),
    )(x)


def expert_work(rows, grads, gate_shard, up_shard, down_shard):
    f32 = jnp.float32
    gate_value = jnp.einsum("trf,tfh->rh", rows, gate_shard, preferred_element_type=f32)
    up_value = jnp.einsum("trf,tfh->rh", rows, up_shard, preferred_element_type=f32)
    sigmoid_value = jax.nn.sigmoid(gate_value)
    silu_value = gate_value * sigmoid_value
    hidden = (silu_value * up_value).astype(jnp.bfloat16)
    hidden_grad = jnp.einsum("trf,htf->rh", grads, down_shard, preferred_element_type=f32)
    gate_grad = (
        hidden_grad * up_value * sigmoid_value * (1.0 + gate_value * (1.0 - sigmoid_value))
    ).astype(jnp.bfloat16)
    up_grad = (hidden_grad * silu_value).astype(jnp.bfloat16)
    row_part = (
        jnp.einsum("rh,tfh->trf", gate_grad, gate_shard, preferred_element_type=f32)
        + jnp.einsum("rh,tfh->trf", up_grad, up_shard, preferred_element_type=f32)
    ).astype(jnp.bfloat16)
    gate_total = jnp.einsum("trf,rh->tfh", rows, gate_grad, preferred_element_type=f32)
    up_total = jnp.einsum("trf,rh->tfh", rows, up_grad, preferred_element_type=f32)
    down_total = jnp.einsum("rh,trf->htf", hidden, grads, preferred_element_type=f32)
    return (
        row_part,
        gate_total.astype(jnp.bfloat16),
        up_total.astype(jnp.bfloat16),
        down_total.astype(jnp.bfloat16),
    )


def shards(tokens, grad_out, expert_ids, gate_probs, w_gate, w_up, w_down):
    dp_size = lax.axis_size("dp")
    tp_size = lax.axis_size("tensor")
    slices = dp_size // EXPERTS
    token_count = tokens.shape[0]
    feat = tokens.shape[1]
    pair_count = token_count * TOP
    flat_ids = expert_ids.reshape(-1)
    experts_row = jnp.arange(EXPERTS, dtype=jnp.int32)
    onehot = (flat_ids[:, None] == experts_row[None, :]).astype(jnp.int32)
    slot_index = jnp.sum((jnp.cumsum(onehot, axis=0) - onehot) * onehot, axis=1)
    positions = jnp.arange(CAP, dtype=jnp.int32)
    matches = (flat_ids[None, None, :] == experts_row[:, None, None]) & (
        slot_index[None, None, :] == positions[None, :, None]
    )
    assignment = jnp.arange(pair_count, dtype=jnp.int32)
    lookup = jnp.sum(jnp.where(matches, assignment[None, None, :], 0), axis=2)
    lookup = lookup + jnp.where(jnp.any(matches, axis=2), 0, pair_count)
    owners = jnp.arange(dp_size, dtype=jnp.int32) // slices
    send_pairs = lookup[owners]
    send_tokens = jnp.where(send_pairs < pair_count, send_pairs // TOP, token_count)
    slice_row = jnp.arange(slices, dtype=jnp.int32)
    back_index = (flat_ids[:, None] * slices + slice_row[None, :]) * CAP + slot_index[:, None]

    bf16 = jnp.bfloat16
    f32 = jnp.float32
    flat_tokens = send_tokens.reshape(-1)
    flat_pairs = send_pairs.reshape(-1)
    pick_tokens = (flat_tokens[:, None] == jnp.arange(token_count)[None, :]).astype(bf16)
    pick_pairs = (flat_pairs[:, None] == assignment[None, :]).astype(bf16)
    scaled = (gate_probs[:, :, None] * grad_out[:, None, :].astype(f32)).astype(bf16)
    sent_rows = jnp.dot(pick_tokens, tokens, preferred_element_type=f32).astype(bf16)
    sent_grads = jnp.dot(pick_pairs, scaled.reshape(pair_count, feat), preferred_element_type=f32)
    sent_grads = sent_grads.astype(bf16)
    rows_count = dp_size * CAP
    sent = jnp.stack(
        [sent_rows.reshape(dp_size, CAP, feat), sent_grads.reshape(dp_size, CAP, feat)], axis=1
    )
    got = dp_all_to_all(sent, dp_size, 0)
    whole_rows = lax.all_gather(got[:, 0].reshape(rows_count, feat), "tensor", axis=0, tiled=True)
    whole_grads = lax.all_gather(
        got[:, 1].reshape(rows_count, feat), "tensor", axis=0, tiled=True
    )
    got_rows = whole_rows.reshape(tp_size, rows_count, feat)
    got_grads = whole_grads.reshape(tp_size, rows_count, feat)
    hid = w_gate.shape[2]
    gate_shard = w_gate[0].reshape(tp_size, feat, hid)
    up_shard = w_up[0].reshape(tp_size, feat, hid)
    down_shard = w_down[0].reshape(hid, tp_size, feat)
    row_part, gate_total, up_total, down_total = expert_work(
        got_rows, got_grads, gate_shard, up_shard, down_shard
    )
    reduced = lax.psum_scatter(row_part, "tensor", scatter_dimension=0, tiled=True)
    reduced, gate_total, up_total, down_total = lax.optimization_barrier(
        (reduced, gate_total, up_total, down_total)
    )
    returned = dp_all_to_all(reduced.reshape(dp_size, CAP, feat), dp_size, 1)
    flat_back = returned.reshape(rows_count, feat)
    back_flat = back_index.reshape(token_count, TOP * slices)
    rows_iota = jnp.arange(rows_count, dtype=jnp.int32)
    gather_back = jnp.sum(
        (back_flat[:, :, None] == rows_iota[None, None, :]).astype(f32), axis=1
    ).astype(bf16)
    input_grad = jnp.dot(gather_back, flat_back, preferred_element_type=f32).astype(bf16)
    return (
        input_grad,
        gate_total.reshape(1, tp_size * feat, hid),
        up_total.reshape(1, tp_size * feat, hid),
        down_total.reshape(1, hid, tp_size * feat),
    )


def solution(mesh):
    placed = (
        P("dp", "tensor"),
        P("dp", "tensor"),
        P("dp", None),
        P("dp", None),
        P("dp", None, "tensor"),
        P("dp", None, "tensor"),
        P("dp", "tensor", None),
    )
    return jax.shard_map(
        shards,
        mesh=mesh,
        in_specs=placed,
        out_specs=(
            P("dp", "tensor"),
            P("dp", None, "tensor"),
            P("dp", None, "tensor"),
            P("dp", "tensor", None),
        ),
        check_vma=False,
    )
```

```python
import functools

import jax
import jax.numpy as jnp
from jax import lax
from jax.experimental import pallas as pl
from jax.experimental.pallas import tpu as pltpu
from jax.sharding import PartitionSpec as P

EXPERTS = 8
TOP = 2
CAP = 33
MESH = pl.DeviceIdType.MESH


def a2a_kernel(n, x_ref, y_ref, send_sem, recv_sem, local_sem):
    me = lax.axis_index("dp")
    tp = lax.axis_index("tensor")
    barrier = pltpu.get_barrier_semaphore()

    def peer(i):
        return lax.rem(me + 1 + i, n)

    def greet(i, carry):
        pl.semaphore_signal(barrier, inc=1, device_id=(peer(i), tp), device_id_type=MESH)
        return carry

    lax.fori_loop(0, n - 1, greet, 0)
    pl.semaphore_wait(barrier, n - 1)
    local = pltpu.make_async_copy(x_ref.at[me], y_ref.at[me], local_sem)
    local.start()

    def outgoing(p):
        return pltpu.make_async_remote_copy(
            src_ref=x_ref.at[p], dst_ref=y_ref.at[me], send_sem=send_sem.at[p],
            recv_sem=recv_sem.at[me], device_id=(p, tp), device_id_type=MESH)

    def incoming(p):
        return pltpu.make_async_remote_copy(
            src_ref=x_ref.at[me], dst_ref=y_ref.at[p], send_sem=send_sem.at[p],
            recv_sem=recv_sem.at[p], device_id=(p, tp), device_id_type=MESH)

    def start(i, carry):
        outgoing(peer(i)).start()
        return carry

    lax.fori_loop(0, n - 1, start, 0)

    def finish(i, carry):
        p = peer(i)
        outgoing(p).wait_send()
        incoming(p).wait_recv()
        return carry

    lax.fori_loop(0, n - 1, finish, 0)
    local.wait()


def dp_all_to_all(x, n, cid):
    return pl.pallas_call(
        functools.partial(a2a_kernel, n),
        out_shape=jax.ShapeDtypeStruct(x.shape, x.dtype),
        in_specs=[pl.BlockSpec(memory_space=pl.ANY)],
        out_specs=pl.BlockSpec(memory_space=pl.ANY),
        scratch_shapes=[
            pltpu.SemaphoreType.DMA((n,)),
            pltpu.SemaphoreType.DMA((n,)),
            pltpu.SemaphoreType.DMA,
        ],
        compiler_params=pltpu.CompilerParams(collective_id=cid, has_side_effects=True),
    )(x)


def expert_work(rows, grads, gate_shard, up_shard, down_shard):
    f32 = jnp.float32
    gate_value = jnp.einsum("trf,tfh->rh", rows, gate_shard, preferred_element_type=f32)
    up_value = jnp.einsum("trf,tfh->rh", rows, up_shard, preferred_element_type=f32)
    sigmoid_value = jax.nn.sigmoid(gate_value)
    silu_value = gate_value * sigmoid_value
    hidden = (silu_value * up_value).astype(jnp.bfloat16)
    hidden_grad = jnp.einsum("trf,htf->rh", grads, down_shard, preferred_element_type=f32)
    gate_grad = (
        hidden_grad * up_value * sigmoid_value * (1.0 + gate_value * (1.0 - sigmoid_value))
    ).astype(jnp.bfloat16)
    up_grad = (hidden_grad * silu_value).astype(jnp.bfloat16)
    row_part = (
        jnp.einsum("rh,tfh->trf", gate_grad, gate_shard, preferred_element_type=f32)
        + jnp.einsum("rh,tfh->trf", up_grad, up_shard, preferred_element_type=f32)
    ).astype(jnp.bfloat16)
    gate_total = jnp.einsum("trf,rh->tfh", rows, gate_grad, preferred_element_type=f32)
    up_total = jnp.einsum("trf,rh->tfh", rows, up_grad, preferred_element_type=f32)
    down_total = jnp.einsum("rh,trf->htf", hidden, grads, preferred_element_type=f32)
    return (row_part, gate_total, up_total, down_total)


def shards(tokens, grad_out, expert_ids, gate_probs, w_gate, w_up, w_down):
    dp_size = lax.axis_size("dp")
    tp_size = lax.axis_size("tensor")
    slices = dp_size // EXPERTS
    token_count = tokens.shape[0]
    feat = tokens.shape[1]
    pair_count = token_count * TOP
    flat_ids = expert_ids.reshape(-1)
    experts_row = jnp.arange(EXPERTS, dtype=jnp.int32)
    onehot = (flat_ids[:, None] == experts_row[None, :]).astype(jnp.int32)
    slot_index = jnp.sum((jnp.cumsum(onehot, axis=0) - onehot) * onehot, axis=1)
    positions = jnp.arange(CAP, dtype=jnp.int32)
    matches = (flat_ids[None, None, :] == experts_row[:, None, None]) & (
        slot_index[None, None, :] == positions[None, :, None]
    )
    assignment = jnp.arange(pair_count, dtype=jnp.int32)
    lookup = jnp.sum(jnp.where(matches, assignment[None, None, :], 0), axis=2)
    lookup = lookup + jnp.where(jnp.any(matches, axis=2), 0, pair_count)
    owners = jnp.arange(dp_size, dtype=jnp.int32) // slices
    send_pairs = lookup[owners]
    send_tokens = jnp.where(send_pairs < pair_count, send_pairs // TOP, token_count)
    slice_row = jnp.arange(slices, dtype=jnp.int32)
    back_index = (flat_ids[:, None] * slices + slice_row[None, :]) * CAP + slot_index[:, None]

    bf16 = jnp.bfloat16
    f32 = jnp.float32
    flat_tokens = send_tokens.reshape(-1)
    flat_pairs = send_pairs.reshape(-1)
    pick_tokens = (flat_tokens[:, None] == jnp.arange(token_count)[None, :]).astype(bf16)
    pick_pairs = (flat_pairs[:, None] == assignment[None, :]).astype(bf16)
    scaled = (gate_probs[:, :, None] * grad_out[:, None, :].astype(f32)).astype(bf16)
    sent_rows = jnp.dot(pick_tokens, tokens, preferred_element_type=f32).astype(bf16)
    sent_grads = jnp.dot(pick_pairs, scaled.reshape(pair_count, feat), preferred_element_type=f32)
    sent_grads = sent_grads.astype(bf16)
    sent = jnp.stack(
        [sent_rows.reshape(dp_size, CAP, feat), sent_grads.reshape(dp_size, CAP, feat)], axis=1
    )
    hid = w_gate.shape[2]
    gate_shard = w_gate[0].reshape(tp_size, feat, hid)
    up_shard = w_up[0].reshape(tp_size, feat, hid)
    down_shard = w_down[0].reshape(hid, tp_size, feat)
    first = (CAP + 1) // 2
    bounds = ((0, first), (first, CAP))
    got = [
        dp_all_to_all(sent[:, :, lo:hi], dp_size, index)
        for index, (lo, hi) in enumerate(bounds)
    ]
    totals = None
    pieces = []
    for index, (lo, hi) in enumerate(bounds):
        rows_count = dp_size * (hi - lo)
        whole_rows = lax.all_gather(
            got[index][:, 0].reshape(rows_count, feat), "tensor", axis=0, tiled=True
        )
        whole_grads = lax.all_gather(
            got[index][:, 1].reshape(rows_count, feat), "tensor", axis=0, tiled=True
        )
        row_part, gate_total, up_total, down_total = expert_work(
            whole_rows.reshape(tp_size, rows_count, feat),
            whole_grads.reshape(tp_size, rows_count, feat),
            gate_shard,
            up_shard,
            down_shard,
        )
        parts = (gate_total, up_total, down_total)
        totals = parts if totals is None else tuple(a + b for a, b in zip(totals, parts))
        reduced = lax.psum_scatter(row_part, "tensor", scatter_dimension=0, tiled=True)
        pieces.append(reduced.reshape(dp_size, hi - lo, feat))
    gate_total, up_total, down_total = (t.astype(bf16) for t in totals)
    returned = [
        dp_all_to_all(piece, dp_size, len(bounds) + index) for index, piece in enumerate(pieces)
    ]
    rows_count = dp_size * CAP
    flat_back = jnp.concatenate(returned, axis=1).reshape(rows_count, feat)
    back_flat = back_index.reshape(token_count, TOP * slices)
    rows_iota = jnp.arange(rows_count, dtype=jnp.int32)
    gather_back = jnp.sum(
        (back_flat[:, :, None] == rows_iota[None, None, :]).astype(f32), axis=1
    ).astype(bf16)
    input_grad = jnp.dot(gather_back, flat_back, preferred_element_type=f32).astype(bf16)
    return (
        input_grad,
        gate_total.reshape(1, tp_size * feat, hid),
        up_total.reshape(1, tp_size * feat, hid),
        down_total.reshape(1, hid, tp_size * feat),
    )


def solution(mesh):
    placed = (
        P("dp", "tensor"),
        P("dp", "tensor"),
        P("dp", None),
        P("dp", None),
        P("dp", None, "tensor"),
        P("dp", None, "tensor"),
        P("dp", "tensor", None),
    )
    return jax.shard_map(
        shards,
        mesh=mesh,
        in_specs=placed,
        out_specs=(
            P("dp", "tensor"),
            P("dp", None, "tensor"),
            P("dp", None, "tensor"),
            P("dp", "tensor", None),
        ),
        check_vma=False,
    )
```

```python
import functools

import jax
import jax.numpy as jnp
from jax import lax
from jax.experimental import pallas as pl
from jax.experimental.pallas import tpu as pltpu
from jax.sharding import PartitionSpec as P

EXPERTS = 8
TOP = 2
CAP = 33
MESH = pl.DeviceIdType.MESH


def a2a_kernel(n, x_ref, y_ref, send_sem, recv_sem, local_sem):
    me = lax.axis_index("dp")
    tp = lax.axis_index("tensor")
    barrier = pltpu.get_barrier_semaphore()

    def peer(i):
        return lax.rem(me + 1 + i, n)

    def greet(i, carry):
        pl.semaphore_signal(barrier, inc=1, device_id=(peer(i), tp), device_id_type=MESH)
        return carry

    lax.fori_loop(0, n - 1, greet, 0)
    pl.semaphore_wait(barrier, n - 1)
    local = pltpu.make_async_copy(x_ref.at[me], y_ref.at[me], local_sem)
    local.start()

    def outgoing(p):
        return pltpu.make_async_remote_copy(
            src_ref=x_ref.at[p], dst_ref=y_ref.at[me], send_sem=send_sem.at[p],
            recv_sem=recv_sem.at[me], device_id=(p, tp), device_id_type=MESH)

    def incoming(p):
        return pltpu.make_async_remote_copy(
            src_ref=x_ref.at[me], dst_ref=y_ref.at[p], send_sem=send_sem.at[p],
            recv_sem=recv_sem.at[p], device_id=(p, tp), device_id_type=MESH)

    def start(i, carry):
        outgoing(peer(i)).start()
        return carry

    lax.fori_loop(0, n - 1, start, 0)

    def finish(i, carry):
        p = peer(i)
        outgoing(p).wait_send()
        incoming(p).wait_recv()
        return carry

    lax.fori_loop(0, n - 1, finish, 0)
    local.wait()


def dp_all_to_all(x, n, cid):
    return pl.pallas_call(
        functools.partial(a2a_kernel, n),
        out_shape=jax.ShapeDtypeStruct(x.shape, x.dtype),
        in_specs=[pl.BlockSpec(memory_space=pl.ANY)],
        out_specs=pl.BlockSpec(memory_space=pl.ANY),
        scratch_shapes=[
            pltpu.SemaphoreType.DMA((n,)),
            pltpu.SemaphoreType.DMA((n,)),
            pltpu.SemaphoreType.DMA,
        ],
        compiler_params=pltpu.CompilerParams(collective_id=cid, has_side_effects=True),
    )(x)


def ag_kernel(n_t, x_ref, y_ref, send_sem, fwd_sem, recv_sem, local_sem):
    dp = lax.axis_index("dp")
    me = lax.axis_index("tensor")
    core = lax.rem(me, 2)
    chip = me // 2
    chips = n_t // 2
    partner = me + 1 - 2 * core
    barrier = pltpu.get_barrier_semaphore()
    targets = [partner] + [2 * lax.rem(chip + k, chips) + core for k in range(1, chips)]
    for target in targets:
        pl.semaphore_signal(barrier, inc=1, device_id=(dp, target), device_id_type=MESH)
    pl.semaphore_wait(barrier, len(targets))
    local = pltpu.make_async_copy(x_ref, y_ref.at[me], local_sem)
    local.start()

    def direct(k, target):
        return pltpu.make_async_remote_copy(
            src_ref=x_ref, dst_ref=y_ref.at[me], send_sem=send_sem.at[k],
            recv_sem=recv_sem.at[me], device_id=(dp, target), device_id_type=MESH)

    for k, target in enumerate(targets):
        direct(k, target).start()

    def arrival(shard):
        return pltpu.make_async_remote_copy(
            src_ref=x_ref, dst_ref=y_ref.at[shard], send_sem=send_sem.at[0],
            recv_sem=recv_sem.at[shard], device_id=(dp, partner), device_id_type=MESH)

    forwards = []
    for k in range(1, chips):
        shard = 2 * lax.rem(chip + chips - k, chips) + core
        arrival(shard).wait_recv()
        forward = pltpu.make_async_remote_copy(
            src_ref=y_ref.at[shard], dst_ref=y_ref.at[shard], send_sem=fwd_sem.at[k - 1],
            recv_sem=recv_sem.at[shard], device_id=(dp, partner), device_id_type=MESH)
        forward.start()
        forwards.append(forward)
    arrival(partner).wait_recv()
    for k in range(1, chips):
        arrival(2 * lax.rem(chip + chips - k, chips) + 1 - core).wait_recv()
    for k, target in enumerate(targets):
        direct(k, target).wait_send()
    for forward in forwards:
        forward.wait_send()
    local.wait()


def tensor_all_gather(x, n_t, cid):
    chips = n_t // 2
    return pl.pallas_call(
        functools.partial(ag_kernel, n_t),
        out_shape=jax.ShapeDtypeStruct((n_t,) + x.shape, x.dtype),
        in_specs=[pl.BlockSpec(memory_space=pl.ANY)],
        out_specs=pl.BlockSpec(memory_space=pl.ANY),
        scratch_shapes=[
            pltpu.SemaphoreType.DMA((chips,)),
            pltpu.SemaphoreType.DMA((chips - 1,)),
            pltpu.SemaphoreType.DMA((n_t,)),
            pltpu.SemaphoreType.DMA,
        ],
        compiler_params=pltpu.CompilerParams(collective_id=cid, has_side_effects=True),
    )(x)


def expert_work(rows, grads, gate_shard, up_shard, down_shard):
    f32 = jnp.float32
    gate_value = jnp.einsum("trf,tfh->rh", rows, gate_shard, preferred_element_type=f32)
    up_value = jnp.einsum("trf,tfh->rh", rows, up_shard, preferred_element_type=f32)
    sigmoid_value = jax.nn.sigmoid(gate_value)
    silu_value = gate_value * sigmoid_value
    hidden = (silu_value * up_value).astype(jnp.bfloat16)
    hidden_grad = jnp.einsum("trf,htf->rh", grads, down_shard, preferred_element_type=f32)
    gate_grad = (
        hidden_grad * up_value * sigmoid_value * (1.0 + gate_value * (1.0 - sigmoid_value))
    ).astype(jnp.bfloat16)
    up_grad = (hidden_grad * silu_value).astype(jnp.bfloat16)
    row_part = (
        jnp.einsum("rh,tfh->trf", gate_grad, gate_shard, preferred_element_type=f32)
        + jnp.einsum("rh,tfh->trf", up_grad, up_shard, preferred_element_type=f32)
    ).astype(jnp.bfloat16)
    gate_total = jnp.einsum("trf,rh->tfh", rows, gate_grad, preferred_element_type=f32)
    up_total = jnp.einsum("trf,rh->tfh", rows, up_grad, preferred_element_type=f32)
    down_total = jnp.einsum("rh,trf->htf", hidden, grads, preferred_element_type=f32)
    return (
        row_part,
        gate_total.astype(jnp.bfloat16),
        up_total.astype(jnp.bfloat16),
        down_total.astype(jnp.bfloat16),
    )


def shards(tokens, grad_out, expert_ids, gate_probs, w_gate, w_up, w_down):
    dp_size = lax.axis_size("dp")
    tp_size = lax.axis_size("tensor")
    slices = dp_size // EXPERTS
    token_count = tokens.shape[0]
    feat = tokens.shape[1]
    pair_count = token_count * TOP
    flat_ids = expert_ids.reshape(-1)
    experts_row = jnp.arange(EXPERTS, dtype=jnp.int32)
    onehot = (flat_ids[:, None] == experts_row[None, :]).astype(jnp.int32)
    slot_index = jnp.sum((jnp.cumsum(onehot, axis=0) - onehot) * onehot, axis=1)
    positions = jnp.arange(CAP, dtype=jnp.int32)
    matches = (flat_ids[None, None, :] == experts_row[:, None, None]) & (
        slot_index[None, None, :] == positions[None, :, None]
    )
    assignment = jnp.arange(pair_count, dtype=jnp.int32)
    lookup = jnp.sum(jnp.where(matches, assignment[None, None, :], 0), axis=2)
    lookup = lookup + jnp.where(jnp.any(matches, axis=2), 0, pair_count)
    owners = jnp.arange(dp_size, dtype=jnp.int32) // slices
    send_pairs = lookup[owners]
    send_tokens = jnp.where(send_pairs < pair_count, send_pairs // TOP, token_count)
    slice_row = jnp.arange(slices, dtype=jnp.int32)
    back_index = (flat_ids[:, None] * slices + slice_row[None, :]) * CAP + slot_index[:, None]

    bf16 = jnp.bfloat16
    f32 = jnp.float32
    flat_tokens = send_tokens.reshape(-1)
    flat_pairs = send_pairs.reshape(-1)
    pick_tokens = (flat_tokens[:, None] == jnp.arange(token_count)[None, :]).astype(bf16)
    pick_pairs = (flat_pairs[:, None] == assignment[None, :]).astype(bf16)
    scaled = (gate_probs[:, :, None] * grad_out[:, None, :].astype(f32)).astype(bf16)
    sent_rows = jnp.dot(pick_tokens, tokens, preferred_element_type=f32).astype(bf16)
    sent_grads = jnp.dot(pick_pairs, scaled.reshape(pair_count, feat), preferred_element_type=f32)
    sent_grads = sent_grads.astype(bf16)
    rows_count = dp_size * CAP
    got_rows = dp_all_to_all(sent_rows.reshape(dp_size, CAP, feat), dp_size, 0)
    got_grads = dp_all_to_all(sent_grads.reshape(dp_size, CAP, feat), dp_size, 1)
    got_rows, got_grads = lax.optimization_barrier((got_rows, got_grads))
    whole_rows = tensor_all_gather(got_rows.reshape(rows_count, feat), tp_size, 3)
    whole_grads = lax.all_gather(
        got_grads.reshape(rows_count, feat), "tensor", axis=0, tiled=True
    )
    got_rows = whole_rows.reshape(tp_size, rows_count, feat)
    got_grads = whole_grads.reshape(tp_size, rows_count, feat)
    hid = w_gate.shape[2]
    gate_shard = w_gate[0].reshape(tp_size, feat, hid)
    up_shard = w_up[0].reshape(tp_size, feat, hid)
    down_shard = w_down[0].reshape(hid, tp_size, feat)
    row_part, gate_total, up_total, down_total = expert_work(
        got_rows, got_grads, gate_shard, up_shard, down_shard
    )
    reduced = lax.psum_scatter(row_part, "tensor", scatter_dimension=0, tiled=True)
    reduced, gate_total, up_total, down_total = lax.optimization_barrier(
        (reduced, gate_total, up_total, down_total)
    )
    returned = dp_all_to_all(reduced.reshape(dp_size, CAP, feat), dp_size, 2)
    flat_back = returned.reshape(rows_count, feat)
    back_flat = back_index.reshape(token_count, TOP * slices)
    rows_iota = jnp.arange(rows_count, dtype=jnp.int32)
    gather_back = jnp.sum(
        (back_flat[:, :, None] == rows_iota[None, None, :]).astype(f32), axis=1
    ).astype(bf16)
    input_grad = jnp.dot(gather_back, flat_back, preferred_element_type=f32).astype(bf16)
    return (
        input_grad,
        gate_total.reshape(1, tp_size * feat, hid),
        up_total.reshape(1, tp_size * feat, hid),
        down_total.reshape(1, hid, tp_size * feat),
    )


def solution(mesh):
    placed = (
        P("dp", "tensor"),
        P("dp", "tensor"),
        P("dp", None),
        P("dp", None),
        P("dp", None, "tensor"),
        P("dp", None, "tensor"),
        P("dp", "tensor", None),
    )
    return jax.shard_map(
        shards,
        mesh=mesh,
        in_specs=placed,
        out_specs=(
            P("dp", "tensor"),
            P("dp", None, "tensor"),
            P("dp", None, "tensor"),
            P("dp", "tensor", None),
        ),
        check_vma=False,
    )
```

```python
import functools

import jax
import jax.numpy as jnp
from jax import lax
from jax.experimental import pallas as pl
from jax.experimental.pallas import tpu as pltpu
from jax.sharding import PartitionSpec as P

EXPERTS = 8
TOP = 2
CAP = 33
MESH = pl.DeviceIdType.MESH


def a2a_kernel(n, x_ref, y_ref, send_sem, recv_sem, local_sem):
    me = lax.axis_index("dp")
    tp = lax.axis_index("tensor")
    barrier = pltpu.get_barrier_semaphore()

    def peer(i):
        return lax.rem(me + 1 + i, n)

    def greet(i, carry):
        pl.semaphore_signal(barrier, inc=1, device_id=(peer(i), tp), device_id_type=MESH)
        return carry

    lax.fori_loop(0, n - 1, greet, 0)
    pl.semaphore_wait(barrier, n - 1)
    local = pltpu.make_async_copy(x_ref.at[me], y_ref.at[me], local_sem)
    local.start()

    def outgoing(p):
        return pltpu.make_async_remote_copy(
            src_ref=x_ref.at[p], dst_ref=y_ref.at[me], send_sem=send_sem.at[p],
            recv_sem=recv_sem.at[me], device_id=(p, tp), device_id_type=MESH)

    def incoming(p):
        return pltpu.make_async_remote_copy(
            src_ref=x_ref.at[me], dst_ref=y_ref.at[p], send_sem=send_sem.at[p],
            recv_sem=recv_sem.at[p], device_id=(p, tp), device_id_type=MESH)

    def start(i, carry):
        outgoing(peer(i)).start()
        return carry

    lax.fori_loop(0, n - 1, start, 0)

    def finish(i, carry):
        p = peer(i)
        outgoing(p).wait_send()
        incoming(p).wait_recv()
        return carry

    lax.fori_loop(0, n - 1, finish, 0)
    local.wait()


def dp_all_to_all(x, n, cid):
    return pl.pallas_call(
        functools.partial(a2a_kernel, n),
        out_shape=jax.ShapeDtypeStruct(x.shape, x.dtype),
        in_specs=[pl.BlockSpec(memory_space=pl.ANY)],
        out_specs=pl.BlockSpec(memory_space=pl.ANY),
        scratch_shapes=[
            pltpu.SemaphoreType.DMA((n,)),
            pltpu.SemaphoreType.DMA((n,)),
            pltpu.SemaphoreType.DMA,
        ],
        compiler_params=pltpu.CompilerParams(collective_id=cid, has_side_effects=True),
    )(x)


def exchange_gather_kernel(n, n_t, g_ref, r_ref, yg_ref, yr_ref,
                           g_send, g_recv, g_local, r_send, r_fwd, r_recv, r_local):
    dp = lax.axis_index("dp")
    me = lax.axis_index("tensor")
    core = lax.rem(me, 2)
    chip = me // 2
    chips = n_t // 2
    partner = me + 1 - 2 * core
    barrier = pltpu.get_barrier_semaphore()
    targets = [partner] + [2 * lax.rem(chip + k, chips) + core for k in range(1, chips)]

    def peer(i):
        return lax.rem(dp + 1 + i, n)

    def greet(i, carry):
        pl.semaphore_signal(barrier, inc=1, device_id=(peer(i), me), device_id_type=MESH)
        return carry

    lax.fori_loop(0, n - 1, greet, 0)
    for target in targets:
        pl.semaphore_signal(barrier, inc=1, device_id=(dp, target), device_id_type=MESH)
    pl.semaphore_wait(barrier, n - 1 + len(targets))

    def outgoing(p):
        return pltpu.make_async_remote_copy(
            src_ref=g_ref.at[p], dst_ref=yg_ref.at[dp], send_sem=g_send.at[p],
            recv_sem=g_recv.at[dp], device_id=(p, me), device_id_type=MESH)

    def incoming(p):
        return pltpu.make_async_remote_copy(
            src_ref=g_ref.at[dp], dst_ref=yg_ref.at[p], send_sem=g_send.at[p],
            recv_sem=g_recv.at[p], device_id=(p, me), device_id_type=MESH)

    def direct(k, target):
        return pltpu.make_async_remote_copy(
            src_ref=r_ref, dst_ref=yr_ref.at[me], send_sem=r_send.at[k],
            recv_sem=r_recv.at[me], device_id=(dp, target), device_id_type=MESH)

    def arrival(shard):
        return pltpu.make_async_remote_copy(
            src_ref=r_ref, dst_ref=yr_ref.at[shard], send_sem=r_send.at[0],
            recv_sem=r_recv.at[shard], device_id=(dp, partner), device_id_type=MESH)

    row_local = pltpu.make_async_copy(r_ref, yr_ref.at[me], r_local)
    row_local.start()
    for k, target in enumerate(targets):
        direct(k, target).start()
    grad_local = pltpu.make_async_copy(g_ref.at[dp], yg_ref.at[dp], g_local)
    grad_local.start()

    def start(i, carry):
        outgoing(peer(i)).start()
        return carry

    lax.fori_loop(0, n - 1, start, 0)
    forwards = []
    for k in range(1, chips):
        shard = 2 * lax.rem(chip + chips - k, chips) + core
        arrival(shard).wait_recv()
        forward = pltpu.make_async_remote_copy(
            src_ref=yr_ref.at[shard], dst_ref=yr_ref.at[shard], send_sem=r_fwd.at[k - 1],
            recv_sem=r_recv.at[shard], device_id=(dp, partner), device_id_type=MESH)
        forward.start()
        forwards.append(forward)
    arrival(partner).wait_recv()
    for k in range(1, chips):
        arrival(2 * lax.rem(chip + chips - k, chips) + 1 - core).wait_recv()

    def finish(i, carry):
        p = peer(i)
        outgoing(p).wait_send()
        incoming(p).wait_recv()
        return carry

    lax.fori_loop(0, n - 1, finish, 0)
    for k, target in enumerate(targets):
        direct(k, target).wait_send()
    for forward in forwards:
        forward.wait_send()
    row_local.wait()
    grad_local.wait()


def exchange_and_gather(grads, rows, n, n_t, cid):
    chips = n_t // 2
    return pl.pallas_call(
        functools.partial(exchange_gather_kernel, n, n_t),
        out_shape=(
            jax.ShapeDtypeStruct(grads.shape, grads.dtype),
            jax.ShapeDtypeStruct((n_t,) + rows.shape, rows.dtype),
        ),
        in_specs=[pl.BlockSpec(memory_space=pl.ANY)] * 2,
        out_specs=(pl.BlockSpec(memory_space=pl.ANY), pl.BlockSpec(memory_space=pl.ANY)),
        scratch_shapes=[
            pltpu.SemaphoreType.DMA((n,)),
            pltpu.SemaphoreType.DMA((n,)),
            pltpu.SemaphoreType.DMA,
            pltpu.SemaphoreType.DMA((chips,)),
            pltpu.SemaphoreType.DMA((chips - 1,)),
            pltpu.SemaphoreType.DMA((n_t,)),
            pltpu.SemaphoreType.DMA,
        ],
        compiler_params=pltpu.CompilerParams(collective_id=cid, has_side_effects=True),
    )(grads, rows)


def expert_work(rows, grads, gate_shard, up_shard, down_shard):
    f32 = jnp.float32
    gate_value = jnp.einsum("trf,tfh->rh", rows, gate_shard, preferred_element_type=f32)
    up_value = jnp.einsum("trf,tfh->rh", rows, up_shard, preferred_element_type=f32)
    sigmoid_value = jax.nn.sigmoid(gate_value)
    silu_value = gate_value * sigmoid_value
    hidden = (silu_value * up_value).astype(jnp.bfloat16)
    hidden_grad = jnp.einsum("trf,htf->rh", grads, down_shard, preferred_element_type=f32)
    gate_grad = (
        hidden_grad * up_value * sigmoid_value * (1.0 + gate_value * (1.0 - sigmoid_value))
    ).astype(jnp.bfloat16)
    up_grad = (hidden_grad * silu_value).astype(jnp.bfloat16)
    row_part = (
        jnp.einsum("rh,tfh->trf", gate_grad, gate_shard, preferred_element_type=f32)
        + jnp.einsum("rh,tfh->trf", up_grad, up_shard, preferred_element_type=f32)
    ).astype(jnp.bfloat16)
    gate_total = jnp.einsum("trf,rh->tfh", rows, gate_grad, preferred_element_type=f32)
    up_total = jnp.einsum("trf,rh->tfh", rows, up_grad, preferred_element_type=f32)
    down_total = jnp.einsum("rh,trf->htf", hidden, grads, preferred_element_type=f32)
    return (
        row_part,
        gate_total.astype(jnp.bfloat16),
        up_total.astype(jnp.bfloat16),
        down_total.astype(jnp.bfloat16),
    )


def shards(tokens, grad_out, expert_ids, gate_probs, w_gate, w_up, w_down):
    dp_size = lax.axis_size("dp")
    tp_size = lax.axis_size("tensor")
    slices = dp_size // EXPERTS
    token_count = tokens.shape[0]
    feat = tokens.shape[1]
    pair_count = token_count * TOP
    flat_ids = expert_ids.reshape(-1)
    experts_row = jnp.arange(EXPERTS, dtype=jnp.int32)
    onehot = (flat_ids[:, None] == experts_row[None, :]).astype(jnp.int32)
    slot_index = jnp.sum((jnp.cumsum(onehot, axis=0) - onehot) * onehot, axis=1)
    positions = jnp.arange(CAP, dtype=jnp.int32)
    matches = (flat_ids[None, None, :] == experts_row[:, None, None]) & (
        slot_index[None, None, :] == positions[None, :, None]
    )
    assignment = jnp.arange(pair_count, dtype=jnp.int32)
    lookup = jnp.sum(jnp.where(matches, assignment[None, None, :], 0), axis=2)
    lookup = lookup + jnp.where(jnp.any(matches, axis=2), 0, pair_count)
    owners = jnp.arange(dp_size, dtype=jnp.int32) // slices
    send_pairs = lookup[owners]
    send_tokens = jnp.where(send_pairs < pair_count, send_pairs // TOP, token_count)
    slice_row = jnp.arange(slices, dtype=jnp.int32)
    back_index = (flat_ids[:, None] * slices + slice_row[None, :]) * CAP + slot_index[:, None]

    bf16 = jnp.bfloat16
    f32 = jnp.float32
    flat_tokens = send_tokens.reshape(-1)
    flat_pairs = send_pairs.reshape(-1)
    pick_tokens = (flat_tokens[:, None] == jnp.arange(token_count)[None, :]).astype(bf16)
    pick_pairs = (flat_pairs[:, None] == assignment[None, :]).astype(bf16)
    scaled = (gate_probs[:, :, None] * grad_out[:, None, :].astype(f32)).astype(bf16)
    sent_rows = jnp.dot(pick_tokens, tokens, preferred_element_type=f32).astype(bf16)
    sent_grads = jnp.dot(pick_pairs, scaled.reshape(pair_count, feat), preferred_element_type=f32)
    sent_grads = sent_grads.astype(bf16)
    rows_count = dp_size * CAP
    got_rows = dp_all_to_all(sent_rows.reshape(dp_size, CAP, feat), dp_size, 0)
    got_grads, whole_rows = exchange_and_gather(
        sent_grads.reshape(dp_size, CAP, feat),
        got_rows.reshape(rows_count, feat),
        dp_size,
        tp_size,
        1,
    )
    whole_grads = lax.all_gather(
        got_grads.reshape(rows_count, feat), "tensor", axis=0, tiled=True
    )
    got_rows = whole_rows.reshape(tp_size, rows_count, feat)
    got_grads = whole_grads.reshape(tp_size, rows_count, feat)
    hid = w_gate.shape[2]
    gate_shard = w_gate[0].reshape(tp_size, feat, hid)
    up_shard = w_up[0].reshape(tp_size, feat, hid)
    down_shard = w_down[0].reshape(hid, tp_size, feat)
    row_part, gate_total, up_total, down_total = expert_work(
        got_rows, got_grads, gate_shard, up_shard, down_shard
    )
    reduced = lax.psum_scatter(row_part, "tensor", scatter_dimension=0, tiled=True)
    reduced, gate_total, up_total, down_total = lax.optimization_barrier(
        (reduced, gate_total, up_total, down_total)
    )
    returned = dp_all_to_all(reduced.reshape(dp_size, CAP, feat), dp_size, 2)
    flat_back = returned.reshape(rows_count, feat)
    back_flat = back_index.reshape(token_count, TOP * slices)
    rows_iota = jnp.arange(rows_count, dtype=jnp.int32)
    gather_back = jnp.sum(
        (back_flat[:, :, None] == rows_iota[None, None, :]).astype(f32), axis=1
    ).astype(bf16)
    input_grad = jnp.dot(gather_back, flat_back, preferred_element_type=f32).astype(bf16)
    return (
        input_grad,
        gate_total.reshape(1, tp_size * feat, hid),
        up_total.reshape(1, tp_size * feat, hid),
        down_total.reshape(1, hid, tp_size * feat),
    )


def solution(mesh):
    placed = (
        P("dp", "tensor"),
        P("dp", "tensor"),
        P("dp", None),
        P("dp", None),
        P("dp", None, "tensor"),
        P("dp", None, "tensor"),
        P("dp", "tensor", None),
    )
    return jax.shard_map(
        shards,
        mesh=mesh,
        in_specs=placed,
        out_specs=(
            P("dp", "tensor"),
            P("dp", None, "tensor"),
            P("dp", None, "tensor"),
            P("dp", "tensor", None),
        ),
        check_vma=False,
    )
```

```python
import functools

import jax
import jax.numpy as jnp
from jax import lax
from jax.experimental import pallas as pl
from jax.experimental.pallas import tpu as pltpu
from jax.sharding import PartitionSpec as P

EXPERTS = 8
TOP = 2
CAP = 33
MESH = pl.DeviceIdType.MESH


def a2a_kernel(n, x_ref, y_ref, send_sem, recv_sem, local_sem):
    me = lax.axis_index("dp")
    tp = lax.axis_index("tensor")
    barrier = pltpu.get_barrier_semaphore()

    def peer(i):
        step = (1 - 2 * lax.rem(i, 2)) * (i // 2 + 1)
        return lax.rem(me + step + n, n)

    def greet(i, carry):
        pl.semaphore_signal(barrier, inc=1, device_id=(peer(i), tp), device_id_type=MESH)
        return carry

    lax.fori_loop(0, n - 1, greet, 0)
    pl.semaphore_wait(barrier, n - 1)
    local = pltpu.make_async_copy(x_ref.at[me], y_ref.at[me], local_sem)
    local.start()

    def outgoing(p):
        return pltpu.make_async_remote_copy(
            src_ref=x_ref.at[p], dst_ref=y_ref.at[me], send_sem=send_sem.at[p],
            recv_sem=recv_sem.at[me], device_id=(p, tp), device_id_type=MESH)

    def incoming(p):
        return pltpu.make_async_remote_copy(
            src_ref=x_ref.at[me], dst_ref=y_ref.at[p], send_sem=send_sem.at[p],
            recv_sem=recv_sem.at[p], device_id=(p, tp), device_id_type=MESH)

    def start(i, carry):
        outgoing(peer(i)).start()
        return carry

    lax.fori_loop(0, n - 1, start, 0)

    def finish(i, carry):
        p = peer(i)
        outgoing(p).wait_send()
        incoming(p).wait_recv()
        return carry

    lax.fori_loop(0, n - 1, finish, 0)
    local.wait()


def dp_all_to_all(x, n, cid):
    return pl.pallas_call(
        functools.partial(a2a_kernel, n),
        out_shape=jax.ShapeDtypeStruct(x.shape, x.dtype),
        in_specs=[pl.BlockSpec(memory_space=pl.ANY)],
        out_specs=pl.BlockSpec(memory_space=pl.ANY),
        scratch_shapes=[
            pltpu.SemaphoreType.DMA((n,)),
            pltpu.SemaphoreType.DMA((n,)),
            pltpu.SemaphoreType.DMA,
        ],
        compiler_params=pltpu.CompilerParams(collective_id=cid, has_side_effects=True),
    )(x)


def exchange_gather_kernel(n, n_t, g_ref, r_ref, yg_ref, yr_ref,
                           g_send, g_recv, g_local, r_send, r_fwd, r_recv, r_local):
    dp = lax.axis_index("dp")
    me = lax.axis_index("tensor")
    core = lax.rem(me, 2)
    chip = me // 2
    chips = n_t // 2
    partner = me + 1 - 2 * core
    barrier = pltpu.get_barrier_semaphore()
    targets = [partner] + [2 * lax.rem(chip + k, chips) + core for k in range(1, chips)]

    def peer(i):
        step = (1 - 2 * lax.rem(i, 2)) * (i // 2 + 1)
        return lax.rem(dp + step + n, n)

    def greet(i, carry):
        pl.semaphore_signal(barrier, inc=1, device_id=(peer(i), me), device_id_type=MESH)
        return carry

    lax.fori_loop(0, n - 1, greet, 0)
    for target in targets:
        pl.semaphore_signal(barrier, inc=1, device_id=(dp, target), device_id_type=MESH)
    pl.semaphore_wait(barrier, n - 1 + len(targets))

    def outgoing(p):
        return pltpu.make_async_remote_copy(
            src_ref=g_ref.at[p], dst_ref=yg_ref.at[dp], send_sem=g_send.at[p],
            recv_sem=g_recv.at[dp], device_id=(p, me), device_id_type=MESH)

    def incoming(p):
        return pltpu.make_async_remote_copy(
            src_ref=g_ref.at[dp], dst_ref=yg_ref.at[p], send_sem=g_send.at[p],
            recv_sem=g_recv.at[p], device_id=(p, me), device_id_type=MESH)

    def direct(k, target):
        return pltpu.make_async_remote_copy(
            src_ref=r_ref, dst_ref=yr_ref.at[me], send_sem=r_send.at[k],
            recv_sem=r_recv.at[me], device_id=(dp, target), device_id_type=MESH)

    def arrival(shard):
        return pltpu.make_async_remote_copy(
            src_ref=r_ref, dst_ref=yr_ref.at[shard], send_sem=r_send.at[0],
            recv_sem=r_recv.at[shard], device_id=(dp, partner), device_id_type=MESH)

    row_local = pltpu.make_async_copy(r_ref, yr_ref.at[me], r_local)
    row_local.start()
    for k, target in enumerate(targets):
        direct(k, target).start()
    grad_local = pltpu.make_async_copy(g_ref.at[dp], yg_ref.at[dp], g_local)
    grad_local.start()

    def start(i, carry):
        outgoing(peer(i)).start()
        return carry

    lax.fori_loop(0, n - 1, start, 0)
    forwards = []
    for k in range(1, chips):
        shard = 2 * lax.rem(chip + chips - k, chips) + core
        arrival(shard).wait_recv()
        forward = pltpu.make_async_remote_copy(
            src_ref=yr_ref.at[shard], dst_ref=yr_ref.at[shard], send_sem=r_fwd.at[k - 1],
            recv_sem=r_recv.at[shard], device_id=(dp, partner), device_id_type=MESH)
        forward.start()
        forwards.append(forward)
    arrival(partner).wait_recv()
    for k in range(1, chips):
        arrival(2 * lax.rem(chip + chips - k, chips) + 1 - core).wait_recv()

    def finish(i, carry):
        p = peer(i)
        outgoing(p).wait_send()
        incoming(p).wait_recv()
        return carry

    lax.fori_loop(0, n - 1, finish, 0)
    for k, target in enumerate(targets):
        direct(k, target).wait_send()
    for forward in forwards:
        forward.wait_send()
    row_local.wait()
    grad_local.wait()


def exchange_and_gather(grads, rows, n, n_t, cid):
    chips = n_t // 2
    return pl.pallas_call(
        functools.partial(exchange_gather_kernel, n, n_t),
        out_shape=(
            jax.ShapeDtypeStruct(grads.shape, grads.dtype),
            jax.ShapeDtypeStruct((n_t,) + rows.shape, rows.dtype),
        ),
        in_specs=[pl.BlockSpec(memory_space=pl.ANY)] * 2,
        out_specs=(pl.BlockSpec(memory_space=pl.ANY), pl.BlockSpec(memory_space=pl.ANY)),
        scratch_shapes=[
            pltpu.SemaphoreType.DMA((n,)),
            pltpu.SemaphoreType.DMA((n,)),
            pltpu.SemaphoreType.DMA,
            pltpu.SemaphoreType.DMA((chips,)),
            pltpu.SemaphoreType.DMA((chips - 1,)),
            pltpu.SemaphoreType.DMA((n_t,)),
            pltpu.SemaphoreType.DMA,
        ],
        compiler_params=pltpu.CompilerParams(collective_id=cid, has_side_effects=True),
    )(grads, rows)


def expert_work(rows, grads, gate_shard, up_shard, down_shard):
    f32 = jnp.float32
    gate_value = jnp.einsum("trf,tfh->rh", rows, gate_shard, preferred_element_type=f32)
    up_value = jnp.einsum("trf,tfh->rh", rows, up_shard, preferred_element_type=f32)
    sigmoid_value = jax.nn.sigmoid(gate_value)
    silu_value = gate_value * sigmoid_value
    hidden = (silu_value * up_value).astype(jnp.bfloat16)
    hidden_grad = jnp.einsum("trf,htf->rh", grads, down_shard, preferred_element_type=f32)
    gate_grad = (
        hidden_grad * up_value * sigmoid_value * (1.0 + gate_value * (1.0 - sigmoid_value))
    ).astype(jnp.bfloat16)
    up_grad = (hidden_grad * silu_value).astype(jnp.bfloat16)
    row_part = (
        jnp.einsum("rh,tfh->trf", gate_grad, gate_shard, preferred_element_type=f32)
        + jnp.einsum("rh,tfh->trf", up_grad, up_shard, preferred_element_type=f32)
    ).astype(jnp.bfloat16)
    gate_total = jnp.einsum("trf,rh->tfh", rows, gate_grad, preferred_element_type=f32)
    up_total = jnp.einsum("trf,rh->tfh", rows, up_grad, preferred_element_type=f32)
    down_total = jnp.einsum("rh,trf->htf", hidden, grads, preferred_element_type=f32)
    return (
        row_part,
        gate_total.astype(jnp.bfloat16),
        up_total.astype(jnp.bfloat16),
        down_total.astype(jnp.bfloat16),
    )


def shards(tokens, grad_out, expert_ids, gate_probs, w_gate, w_up, w_down):
    dp_size = lax.axis_size("dp")
    tp_size = lax.axis_size("tensor")
    slices = dp_size // EXPERTS
    token_count = tokens.shape[0]
    feat = tokens.shape[1]
    pair_count = token_count * TOP
    flat_ids = expert_ids.reshape(-1)
    experts_row = jnp.arange(EXPERTS, dtype=jnp.int32)
    onehot = (flat_ids[:, None] == experts_row[None, :]).astype(jnp.int32)
    slot_index = jnp.sum((jnp.cumsum(onehot, axis=0) - onehot) * onehot, axis=1)
    positions = jnp.arange(CAP, dtype=jnp.int32)
    matches = (flat_ids[None, None, :] == experts_row[:, None, None]) & (
        slot_index[None, None, :] == positions[None, :, None]
    )
    assignment = jnp.arange(pair_count, dtype=jnp.int32)
    lookup = jnp.sum(jnp.where(matches, assignment[None, None, :], 0), axis=2)
    lookup = lookup + jnp.where(jnp.any(matches, axis=2), 0, pair_count)
    owners = jnp.arange(dp_size, dtype=jnp.int32) // slices
    send_pairs = lookup[owners]
    send_tokens = jnp.where(send_pairs < pair_count, send_pairs // TOP, token_count)
    slice_row = jnp.arange(slices, dtype=jnp.int32)
    back_index = (flat_ids[:, None] * slices + slice_row[None, :]) * CAP + slot_index[:, None]

    bf16 = jnp.bfloat16
    f32 = jnp.float32
    flat_tokens = send_tokens.reshape(-1)
    flat_pairs = send_pairs.reshape(-1)
    pick_tokens = (flat_tokens[:, None] == jnp.arange(token_count)[None, :]).astype(bf16)
    pick_pairs = (flat_pairs[:, None] == assignment[None, :]).astype(bf16)
    scaled = (gate_probs[:, :, None] * grad_out[:, None, :].astype(f32)).astype(bf16)
    sent_rows = jnp.dot(pick_tokens, tokens, preferred_element_type=f32).astype(bf16)
    sent_grads = jnp.dot(pick_pairs, scaled.reshape(pair_count, feat), preferred_element_type=f32)
    sent_grads = sent_grads.astype(bf16)
    rows_count = dp_size * CAP
    got_rows = dp_all_to_all(sent_rows.reshape(dp_size, CAP, feat), dp_size, 0)
    got_grads, whole_rows = exchange_and_gather(
        sent_grads.reshape(dp_size, CAP, feat),
        got_rows.reshape(rows_count, feat),
        dp_size,
        tp_size,
        1,
    )
    whole_grads = lax.all_gather(
        got_grads.reshape(rows_count, feat), "tensor", axis=0, tiled=True
    )
    got_rows = whole_rows.reshape(tp_size, rows_count, feat)
    got_grads = whole_grads.reshape(tp_size, rows_count, feat)
    hid = w_gate.shape[2]
    gate_shard = w_gate[0].reshape(tp_size, feat, hid)
    up_shard = w_up[0].reshape(tp_size, feat, hid)
    down_shard = w_down[0].reshape(hid, tp_size, feat)
    row_part, gate_total, up_total, down_total = expert_work(
        got_rows, got_grads, gate_shard, up_shard, down_shard
    )
    reduced = lax.psum_scatter(row_part, "tensor", scatter_dimension=0, tiled=True)
    reduced, gate_total, up_total, down_total = lax.optimization_barrier(
        (reduced, gate_total, up_total, down_total)
    )
    returned = dp_all_to_all(reduced.reshape(dp_size, CAP, feat), dp_size, 2)
    flat_back = returned.reshape(rows_count, feat)
    back_flat = back_index.reshape(token_count, TOP * slices)
    rows_iota = jnp.arange(rows_count, dtype=jnp.int32)
    gather_back = jnp.sum(
        (back_flat[:, :, None] == rows_iota[None, None, :]).astype(f32), axis=1
    ).astype(bf16)
    input_grad = jnp.dot(gather_back, flat_back, preferred_element_type=f32).astype(bf16)
    return (
        input_grad,
        gate_total.reshape(1, tp_size * feat, hid),
        up_total.reshape(1, tp_size * feat, hid),
        down_total.reshape(1, hid, tp_size * feat),
    )


def solution(mesh):
    placed = (
        P("dp", "tensor"),
        P("dp", "tensor"),
        P("dp", None),
        P("dp", None),
        P("dp", None, "tensor"),
        P("dp", None, "tensor"),
        P("dp", "tensor", None),
    )
    return jax.shard_map(
        shards,
        mesh=mesh,
        in_specs=placed,
        out_specs=(
            P("dp", "tensor"),
            P("dp", None, "tensor"),
            P("dp", None, "tensor"),
            P("dp", "tensor", None),
        ),
        check_vma=False,
    )
```

```python
import functools

import jax
import jax.numpy as jnp
from jax import lax
from jax.experimental import pallas as pl
from jax.experimental.pallas import tpu as pltpu
from jax.sharding import PartitionSpec as P

EXPERTS = 8
TOP = 2
CAP = 33
MESH = pl.DeviceIdType.MESH


def a2a_kernel(n, x_ref, y_ref, send_sem, recv_sem, local_sem):
    me = lax.axis_index("dp")
    tp = lax.axis_index("tensor")
    barrier = pltpu.get_barrier_semaphore()

    def peer(i):
        return lax.rem(me + 1 + i, n)

    def greet(i, carry):
        pl.semaphore_signal(barrier, inc=1, device_id=(peer(i), tp), device_id_type=MESH)
        return carry

    lax.fori_loop(0, n - 1, greet, 0)
    pl.semaphore_wait(barrier, n - 1)
    local = pltpu.make_async_copy(x_ref.at[me], y_ref.at[me], local_sem)
    local.start()

    def outgoing(p):
        return pltpu.make_async_remote_copy(
            src_ref=x_ref.at[p], dst_ref=y_ref.at[me], send_sem=send_sem.at[p],
            recv_sem=recv_sem.at[me], device_id=(p, tp), device_id_type=MESH)

    def incoming(p):
        return pltpu.make_async_remote_copy(
            src_ref=x_ref.at[me], dst_ref=y_ref.at[p], send_sem=send_sem.at[p],
            recv_sem=recv_sem.at[p], device_id=(p, tp), device_id_type=MESH)

    def start(i, carry):
        outgoing(peer(i)).start()
        return carry

    lax.fori_loop(0, n - 1, start, 0)

    def finish(i, carry):
        p = peer(i)
        outgoing(p).wait_send()
        incoming(p).wait_recv()
        return carry

    lax.fori_loop(0, n - 1, finish, 0)
    local.wait()


def dp_all_to_all(x, n, cid):
    return pl.pallas_call(
        functools.partial(a2a_kernel, n),
        out_shape=jax.ShapeDtypeStruct(x.shape, x.dtype),
        in_specs=[pl.BlockSpec(memory_space=pl.ANY)],
        out_specs=pl.BlockSpec(memory_space=pl.ANY),
        scratch_shapes=[
            pltpu.SemaphoreType.DMA((n,)),
            pltpu.SemaphoreType.DMA((n,)),
            pltpu.SemaphoreType.DMA,
        ],
        compiler_params=pltpu.CompilerParams(collective_id=cid, has_side_effects=True),
    )(x)


def exchange_gather_kernel(n, n_t, g_ref, r_ref, yg_ref, yr_ref,
                           g_send, g_recv, g_local, r_send, r_fwd, r_recv, r_local):
    dp = lax.axis_index("dp")
    me = lax.axis_index("tensor")
    core = lax.rem(me, 2)
    chip = me // 2
    chips = n_t // 2
    partner = me + 1 - 2 * core
    barrier = pltpu.get_barrier_semaphore()
    targets = [partner] + [2 * lax.rem(chip + k, chips) + core for k in range(1, chips)]

    def peer(i):
        return lax.rem(dp + 1 + i, n)

    def greet(i, carry):
        pl.semaphore_signal(barrier, inc=1, device_id=(peer(i), me), device_id_type=MESH)
        return carry

    lax.fori_loop(0, n - 1, greet, 0)
    for target in targets:
        pl.semaphore_signal(barrier, inc=1, device_id=(dp, target), device_id_type=MESH)
    pl.semaphore_wait(barrier, n - 1 + len(targets))

    def outgoing(p):
        return pltpu.make_async_remote_copy(
            src_ref=g_ref.at[p], dst_ref=yg_ref.at[dp], send_sem=g_send.at[p],
            recv_sem=g_recv.at[dp], device_id=(p, me), device_id_type=MESH)

    def incoming(p):
        return pltpu.make_async_remote_copy(
            src_ref=g_ref.at[dp], dst_ref=yg_ref.at[p], send_sem=g_send.at[p],
            recv_sem=g_recv.at[p], device_id=(p, me), device_id_type=MESH)

    def direct(k, target):
        return pltpu.make_async_remote_copy(
            src_ref=r_ref, dst_ref=yr_ref.at[me], send_sem=r_send.at[k],
            recv_sem=r_recv.at[me], device_id=(dp, target), device_id_type=MESH)

    def arrival(shard):
        return pltpu.make_async_remote_copy(
            src_ref=r_ref, dst_ref=yr_ref.at[shard], send_sem=r_send.at[0],
            recv_sem=r_recv.at[shard], device_id=(dp, partner), device_id_type=MESH)

    row_local = pltpu.make_async_copy(r_ref, yr_ref.at[me], r_local)
    row_local.start()
    for k, target in enumerate(targets):
        direct(k, target).start()
    grad_local = pltpu.make_async_copy(g_ref.at[dp], yg_ref.at[dp], g_local)
    grad_local.start()

    def start(i, carry):
        outgoing(peer(i)).start()
        return carry

    lax.fori_loop(0, n - 1, start, 0)
    forwards = []
    for k in range(1, chips):
        shard = 2 * lax.rem(chip + chips - k, chips) + core
        arrival(shard).wait_recv()
        forward = pltpu.make_async_remote_copy(
            src_ref=yr_ref.at[shard], dst_ref=yr_ref.at[shard], send_sem=r_fwd.at[k - 1],
            recv_sem=r_recv.at[shard], device_id=(dp, partner), device_id_type=MESH)
        forward.start()
        forwards.append(forward)
    arrival(partner).wait_recv()
    for k in range(1, chips):
        arrival(2 * lax.rem(chip + chips - k, chips) + 1 - core).wait_recv()

    def finish(i, carry):
        p = peer(i)
        outgoing(p).wait_send()
        incoming(p).wait_recv()
        return carry

    lax.fori_loop(0, n - 1, finish, 0)
    for k, target in enumerate(targets):
        direct(k, target).wait_send()
    for forward in forwards:
        forward.wait_send()
    row_local.wait()
    grad_local.wait()


def exchange_and_gather(grads, rows, n, n_t, cid):
    chips = n_t // 2
    return pl.pallas_call(
        functools.partial(exchange_gather_kernel, n, n_t),
        out_shape=(
            jax.ShapeDtypeStruct(grads.shape, grads.dtype),
            jax.ShapeDtypeStruct((n_t,) + rows.shape, rows.dtype),
        ),
        in_specs=[pl.BlockSpec(memory_space=pl.ANY)] * 2,
        out_specs=(pl.BlockSpec(memory_space=pl.ANY), pl.BlockSpec(memory_space=pl.ANY)),
        scratch_shapes=[
            pltpu.SemaphoreType.DMA((n,)),
            pltpu.SemaphoreType.DMA((n,)),
            pltpu.SemaphoreType.DMA,
            pltpu.SemaphoreType.DMA((chips,)),
            pltpu.SemaphoreType.DMA((chips - 1,)),
            pltpu.SemaphoreType.DMA((n_t,)),
            pltpu.SemaphoreType.DMA,
        ],
        compiler_params=pltpu.CompilerParams(collective_id=cid, has_side_effects=True),
    )(grads, rows)


def ag_kernel(n_t, x_ref, y_ref, send_sem, fwd_sem, recv_sem, local_sem):
    dp = lax.axis_index("dp")
    me = lax.axis_index("tensor")
    core = lax.rem(me, 2)
    chip = me // 2
    chips = n_t // 2
    partner = me + 1 - 2 * core
    barrier = pltpu.get_barrier_semaphore()
    targets = [partner] + [2 * lax.rem(chip + k, chips) + core for k in range(1, chips)]
    for target in targets:
        pl.semaphore_signal(barrier, inc=1, device_id=(dp, target), device_id_type=MESH)
    pl.semaphore_wait(barrier, len(targets))
    local = pltpu.make_async_copy(x_ref, y_ref.at[me], local_sem)
    local.start()

    def direct(k, target):
        return pltpu.make_async_remote_copy(
            src_ref=x_ref, dst_ref=y_ref.at[me], send_sem=send_sem.at[k],
            recv_sem=recv_sem.at[me], device_id=(dp, target), device_id_type=MESH)

    for k, target in enumerate(targets):
        direct(k, target).start()

    def arrival(shard):
        return pltpu.make_async_remote_copy(
            src_ref=x_ref, dst_ref=y_ref.at[shard], send_sem=send_sem.at[0],
            recv_sem=recv_sem.at[shard], device_id=(dp, partner), device_id_type=MESH)

    forwards = []
    for k in range(1, chips):
        shard = 2 * lax.rem(chip + chips - k, chips) + core
        arrival(shard).wait_recv()
        forward = pltpu.make_async_remote_copy(
            src_ref=y_ref.at[shard], dst_ref=y_ref.at[shard], send_sem=fwd_sem.at[k - 1],
            recv_sem=recv_sem.at[shard], device_id=(dp, partner), device_id_type=MESH)
        forward.start()
        forwards.append(forward)
    arrival(partner).wait_recv()
    for k in range(1, chips):
        arrival(2 * lax.rem(chip + chips - k, chips) + 1 - core).wait_recv()
    for k, target in enumerate(targets):
        direct(k, target).wait_send()
    for forward in forwards:
        forward.wait_send()
    local.wait()


def tensor_all_gather(x, n_t, cid):
    chips = n_t // 2
    return pl.pallas_call(
        functools.partial(ag_kernel, n_t),
        out_shape=jax.ShapeDtypeStruct((n_t,) + x.shape, x.dtype),
        in_specs=[pl.BlockSpec(memory_space=pl.ANY)],
        out_specs=pl.BlockSpec(memory_space=pl.ANY),
        scratch_shapes=[
            pltpu.SemaphoreType.DMA((chips,)),
            pltpu.SemaphoreType.DMA((chips - 1,)),
            pltpu.SemaphoreType.DMA((n_t,)),
            pltpu.SemaphoreType.DMA,
        ],
        compiler_params=pltpu.CompilerParams(collective_id=cid, has_side_effects=True),
    )(x)


def expert_work(rows, grads, gate_shard, up_shard, down_shard):
    f32 = jnp.float32
    gate_value = jnp.einsum("trf,tfh->rh", rows, gate_shard, preferred_element_type=f32)
    up_value = jnp.einsum("trf,tfh->rh", rows, up_shard, preferred_element_type=f32)
    sigmoid_value = jax.nn.sigmoid(gate_value)
    silu_value = gate_value * sigmoid_value
    hidden = (silu_value * up_value).astype(jnp.bfloat16)
    hidden_grad = jnp.einsum("trf,htf->rh", grads, down_shard, preferred_element_type=f32)
    gate_grad = (
        hidden_grad * up_value * sigmoid_value * (1.0 + gate_value * (1.0 - sigmoid_value))
    ).astype(jnp.bfloat16)
    up_grad = (hidden_grad * silu_value).astype(jnp.bfloat16)
    row_part = (
        jnp.einsum("rh,tfh->trf", gate_grad, gate_shard, preferred_element_type=f32)
        + jnp.einsum("rh,tfh->trf", up_grad, up_shard, preferred_element_type=f32)
    ).astype(jnp.bfloat16)
    gate_total = jnp.einsum("trf,rh->tfh", rows, gate_grad, preferred_element_type=f32)
    up_total = jnp.einsum("trf,rh->tfh", rows, up_grad, preferred_element_type=f32)
    down_total = jnp.einsum("rh,trf->htf", hidden, grads, preferred_element_type=f32)
    return (
        row_part,
        gate_total.astype(jnp.bfloat16),
        up_total.astype(jnp.bfloat16),
        down_total.astype(jnp.bfloat16),
    )


def shards(tokens, grad_out, expert_ids, gate_probs, w_gate, w_up, w_down):
    dp_size = lax.axis_size("dp")
    tp_size = lax.axis_size("tensor")
    slices = dp_size // EXPERTS
    token_count = tokens.shape[0]
    feat = tokens.shape[1]
    pair_count = token_count * TOP
    flat_ids = expert_ids.reshape(-1)
    experts_row = jnp.arange(EXPERTS, dtype=jnp.int32)
    onehot = (flat_ids[:, None] == experts_row[None, :]).astype(jnp.int32)
    slot_index = jnp.sum((jnp.cumsum(onehot, axis=0) - onehot) * onehot, axis=1)
    positions = jnp.arange(CAP, dtype=jnp.int32)
    matches = (flat_ids[None, None, :] == experts_row[:, None, None]) & (
        slot_index[None, None, :] == positions[None, :, None]
    )
    assignment = jnp.arange(pair_count, dtype=jnp.int32)
    lookup = jnp.sum(jnp.where(matches, assignment[None, None, :], 0), axis=2)
    lookup = lookup + jnp.where(jnp.any(matches, axis=2), 0, pair_count)
    owners = jnp.arange(dp_size, dtype=jnp.int32) // slices
    send_pairs = lookup[owners]
    send_tokens = jnp.where(send_pairs < pair_count, send_pairs // TOP, token_count)
    slice_row = jnp.arange(slices, dtype=jnp.int32)
    back_index = (flat_ids[:, None] * slices + slice_row[None, :]) * CAP + slot_index[:, None]

    bf16 = jnp.bfloat16
    f32 = jnp.float32
    flat_tokens = send_tokens.reshape(-1)
    flat_pairs = send_pairs.reshape(-1)
    pick_tokens = (flat_tokens[:, None] == jnp.arange(token_count)[None, :]).astype(bf16)
    pick_pairs = (flat_pairs[:, None] == assignment[None, :]).astype(bf16)
    scaled = (gate_probs[:, :, None] * grad_out[:, None, :].astype(f32)).astype(bf16)
    sent_rows = jnp.dot(pick_tokens, tokens, preferred_element_type=f32).astype(bf16)
    sent_grads = jnp.dot(pick_pairs, scaled.reshape(pair_count, feat), preferred_element_type=f32)
    sent_grads = sent_grads.astype(bf16)
    rows_count = dp_size * CAP
    got_rows = dp_all_to_all(sent_rows.reshape(dp_size, CAP, feat), dp_size, 0)
    got_grads, whole_rows = exchange_and_gather(
        sent_grads.reshape(dp_size, CAP, feat),
        got_rows.reshape(rows_count, feat),
        dp_size,
        tp_size,
        1,
    )
    whole_grads = tensor_all_gather(got_grads.reshape(rows_count, feat), tp_size, 3)
    got_rows = whole_rows.reshape(tp_size, rows_count, feat)
    got_grads = whole_grads.reshape(tp_size, rows_count, feat)
    hid = w_gate.shape[2]
    gate_shard = w_gate[0].reshape(tp_size, feat, hid)
    up_shard = w_up[0].reshape(tp_size, feat, hid)
    down_shard = w_down[0].reshape(hid, tp_size, feat)
    row_part, gate_total, up_total, down_total = expert_work(
        got_rows, got_grads, gate_shard, up_shard, down_shard
    )
    reduced = lax.psum_scatter(row_part, "tensor", scatter_dimension=0, tiled=True)
    reduced, gate_total, up_total, down_total = lax.optimization_barrier(
        (reduced, gate_total, up_total, down_total)
    )
    returned = dp_all_to_all(reduced.reshape(dp_size, CAP, feat), dp_size, 2)
    flat_back = returned.reshape(rows_count, feat)
    back_flat = back_index.reshape(token_count, TOP * slices)
    rows_iota = jnp.arange(rows_count, dtype=jnp.int32)
    gather_back = jnp.sum(
        (back_flat[:, :, None] == rows_iota[None, None, :]).astype(f32), axis=1
    ).astype(bf16)
    input_grad = jnp.dot(gather_back, flat_back, preferred_element_type=f32).astype(bf16)
    return (
        input_grad,
        gate_total.reshape(1, tp_size * feat, hid),
        up_total.reshape(1, tp_size * feat, hid),
        down_total.reshape(1, hid, tp_size * feat),
    )


def solution(mesh):
    placed = (
        P("dp", "tensor"),
        P("dp", "tensor"),
        P("dp", None),
        P("dp", None),
        P("dp", None, "tensor"),
        P("dp", None, "tensor"),
        P("dp", "tensor", None),
    )
    return jax.shard_map(
        shards,
        mesh=mesh,
        in_specs=placed,
        out_specs=(
            P("dp", "tensor"),
            P("dp", None, "tensor"),
            P("dp", None, "tensor"),
            P("dp", "tensor", None),
        ),
        check_vma=False,
    )
```

```python
import functools

import jax
import jax.numpy as jnp
from jax import lax
from jax.experimental import pallas as pl
from jax.experimental.pallas import tpu as pltpu
from jax.sharding import PartitionSpec as P

EXPERTS = 8
TOP = 2
CAP = 33
MESH = pl.DeviceIdType.MESH


def a2a_kernel(n, x_ref, y_ref, send_sem, recv_sem, local_sem):
    me = lax.axis_index("dp")
    tp = lax.axis_index("tensor")
    barrier = pltpu.get_barrier_semaphore()

    def peer(i):
        return lax.rem(me + 1 + i, n)

    def greet(i, carry):
        pl.semaphore_signal(barrier, inc=1, device_id=(peer(i), tp), device_id_type=MESH)
        return carry

    lax.fori_loop(0, n - 1, greet, 0)
    pl.semaphore_wait(barrier, n - 1)
    local = pltpu.make_async_copy(x_ref.at[me], y_ref.at[me], local_sem)
    local.start()

    def outgoing(p):
        return pltpu.make_async_remote_copy(
            src_ref=x_ref.at[p], dst_ref=y_ref.at[me], send_sem=send_sem.at[p],
            recv_sem=recv_sem.at[me], device_id=(p, tp), device_id_type=MESH)

    def incoming(p):
        return pltpu.make_async_remote_copy(
            src_ref=x_ref.at[me], dst_ref=y_ref.at[p], send_sem=send_sem.at[p],
            recv_sem=recv_sem.at[p], device_id=(p, tp), device_id_type=MESH)

    def start(i, carry):
        outgoing(peer(i)).start()
        return carry

    lax.fori_loop(0, n - 1, start, 0)

    def finish(i, carry):
        p = peer(i)
        outgoing(p).wait_send()
        incoming(p).wait_recv()
        return carry

    lax.fori_loop(0, n - 1, finish, 0)
    local.wait()


def dp_all_to_all(x, n, cid):
    return pl.pallas_call(
        functools.partial(a2a_kernel, n),
        out_shape=jax.ShapeDtypeStruct(x.shape, x.dtype),
        in_specs=[pl.BlockSpec(memory_space=pl.ANY)],
        out_specs=pl.BlockSpec(memory_space=pl.ANY),
        scratch_shapes=[
            pltpu.SemaphoreType.DMA((n,)),
            pltpu.SemaphoreType.DMA((n,)),
            pltpu.SemaphoreType.DMA,
        ],
        compiler_params=pltpu.CompilerParams(collective_id=cid, has_side_effects=True),
    )(x)


def expert_work(rows, grads, gate_shard, up_shard, down_shard):
    f32 = jnp.float32
    gate_value = jnp.einsum("trf,tfh->rh", rows, gate_shard, preferred_element_type=f32)
    up_value = jnp.einsum("trf,tfh->rh", rows, up_shard, preferred_element_type=f32)
    sigmoid_value = jax.nn.sigmoid(gate_value)
    silu_value = gate_value * sigmoid_value
    hidden = (silu_value * up_value).astype(jnp.bfloat16)
    hidden_grad = jnp.einsum("trf,htf->rh", grads, down_shard, preferred_element_type=f32)
    gate_grad = (
        hidden_grad * up_value * sigmoid_value * (1.0 + gate_value * (1.0 - sigmoid_value))
    ).astype(jnp.bfloat16)
    up_grad = (hidden_grad * silu_value).astype(jnp.bfloat16)
    row_part = (
        jnp.einsum("rh,tfh->trf", gate_grad, gate_shard, preferred_element_type=f32)
        + jnp.einsum("rh,tfh->trf", up_grad, up_shard, preferred_element_type=f32)
    ).astype(jnp.bfloat16)
    gate_total = jnp.einsum("trf,rh->tfh", rows, gate_grad, preferred_element_type=f32)
    up_total = jnp.einsum("trf,rh->tfh", rows, up_grad, preferred_element_type=f32)
    down_total = jnp.einsum("rh,trf->htf", hidden, grads, preferred_element_type=f32)
    return (
        row_part,
        gate_total.astype(jnp.bfloat16),
        up_total.astype(jnp.bfloat16),
        down_total.astype(jnp.bfloat16),
    )


def shards(tokens, grad_out, expert_ids, gate_probs, w_gate, w_up, w_down):
    dp_size = lax.axis_size("dp")
    tp_size = lax.axis_size("tensor")
    slices = dp_size // EXPERTS
    token_count = tokens.shape[0]
    feat = tokens.shape[1]
    pair_count = token_count * TOP
    flat_ids = expert_ids.reshape(-1)
    experts_row = jnp.arange(EXPERTS, dtype=jnp.int32)
    onehot = (flat_ids[:, None] == experts_row[None, :]).astype(jnp.int32)
    slot_index = jnp.sum((jnp.cumsum(onehot, axis=0) - onehot) * onehot, axis=1)
    positions = jnp.arange(CAP, dtype=jnp.int32)
    matches = (flat_ids[None, None, :] == experts_row[:, None, None]) & (
        slot_index[None, None, :] == positions[None, :, None]
    )
    assignment = jnp.arange(pair_count, dtype=jnp.int32)
    lookup = jnp.sum(jnp.where(matches, assignment[None, None, :], 0), axis=2)
    lookup = lookup + jnp.where(jnp.any(matches, axis=2), 0, pair_count)
    owners = jnp.arange(dp_size, dtype=jnp.int32) // slices
    send_pairs = lookup[owners]
    send_tokens = jnp.where(send_pairs < pair_count, send_pairs // TOP, token_count)
    slice_row = jnp.arange(slices, dtype=jnp.int32)
    back_index = (flat_ids[:, None] * slices + slice_row[None, :]) * CAP + slot_index[:, None]

    bf16 = jnp.bfloat16
    f32 = jnp.float32
    flat_tokens = send_tokens.reshape(-1)
    flat_pairs = send_pairs.reshape(-1)
    pick_tokens = (send_tokens[:, :, None] == jnp.arange(token_count)[None, None, :]).astype(bf16)
    pick_pairs = (send_pairs[:, :, None] == assignment[None, None, :]).astype(bf16)
    scaled = (gate_probs[:, :, None] * grad_out[:, None, :].astype(f32)).astype(bf16)
    sent_rows = jnp.einsum("pcn,nf->pcf", pick_tokens, tokens, preferred_element_type=f32)
    sent_grads = jnp.einsum(
        "pcn,nf->pcf", pick_pairs, scaled.reshape(pair_count, feat), preferred_element_type=f32
    )
    rows_count = dp_size * CAP
    got_rows = dp_all_to_all(sent_rows.astype(bf16), dp_size, 0)
    whole_rows = lax.all_gather(got_rows.reshape(rows_count, feat), "tensor", axis=0, tiled=True)
    got_grads = dp_all_to_all(sent_grads.astype(bf16), dp_size, 1)
    whole_grads = lax.all_gather(
        got_grads.reshape(rows_count, feat), "tensor", axis=0, tiled=True
    )
    got_rows = whole_rows.reshape(tp_size, rows_count, feat)
    got_grads = whole_grads.reshape(tp_size, rows_count, feat)
    hid = w_gate.shape[2]
    gate_shard = w_gate[0].reshape(tp_size, feat, hid)
    up_shard = w_up[0].reshape(tp_size, feat, hid)
    down_shard = w_down[0].reshape(hid, tp_size, feat)
    row_part, gate_total, up_total, down_total = expert_work(
        got_rows, got_grads, gate_shard, up_shard, down_shard
    )
    reduced = lax.psum_scatter(row_part, "tensor", scatter_dimension=0, tiled=True)
    reduced, gate_total, up_total, down_total = lax.optimization_barrier(
        (reduced, gate_total, up_total, down_total)
    )
    returned = dp_all_to_all(reduced.reshape(dp_size, CAP, feat), dp_size, 2)
    back_flat = back_index.reshape(token_count, TOP * slices)
    rows_iota = jnp.arange(rows_count, dtype=jnp.int32).reshape(dp_size, CAP)
    gather_back = jnp.sum(
        (back_flat[:, :, None, None] == rows_iota[None, None, :, :]).astype(f32), axis=1
    ).astype(bf16)
    input_grad = jnp.einsum(
        "npc,pcf->nf", gather_back, returned, preferred_element_type=f32
    ).astype(bf16)
    return (
        input_grad,
        gate_total.reshape(1, tp_size * feat, hid),
        up_total.reshape(1, tp_size * feat, hid),
        down_total.reshape(1, hid, tp_size * feat),
    )


def solution(mesh):
    placed = (
        P("dp", "tensor"),
        P("dp", "tensor"),
        P("dp", None),
        P("dp", None),
        P("dp", None, "tensor"),
        P("dp", None, "tensor"),
        P("dp", "tensor", None),
    )
    return jax.shard_map(
        shards,
        mesh=mesh,
        in_specs=placed,
        out_specs=(
            P("dp", "tensor"),
            P("dp", None, "tensor"),
            P("dp", None, "tensor"),
            P("dp", "tensor", None),
        ),
        check_vma=False,
    )
```

```python
import functools

import jax
import jax.numpy as jnp
from jax import lax
from jax.experimental import pallas as pl
from jax.experimental.pallas import tpu as pltpu
from jax.sharding import PartitionSpec as P

EXPERTS = 8
TOP = 2
CAP = 33
MESH = pl.DeviceIdType.MESH


def a2a_kernel(n, x_ref, y_ref, send_sem, recv_sem, local_sem):
    me = lax.axis_index("dp")
    tp = lax.axis_index("tensor")
    barrier = pltpu.get_barrier_semaphore()

    def peer(i):
        return lax.rem(me + 1 + i, n)

    def greet(i, carry):
        pl.semaphore_signal(barrier, inc=1, device_id=(peer(i), tp), device_id_type=MESH)
        return carry

    lax.fori_loop(0, n - 1, greet, 0)
    pl.semaphore_wait(barrier, n - 1)
    local = pltpu.make_async_copy(x_ref.at[me], y_ref.at[me], local_sem)
    local.start()

    def outgoing(p):
        return pltpu.make_async_remote_copy(
            src_ref=x_ref.at[p], dst_ref=y_ref.at[me], send_sem=send_sem.at[p],
            recv_sem=recv_sem.at[me], device_id=(p, tp), device_id_type=MESH)

    def incoming(p):
        return pltpu.make_async_remote_copy(
            src_ref=x_ref.at[me], dst_ref=y_ref.at[p], send_sem=send_sem.at[p],
            recv_sem=recv_sem.at[p], device_id=(p, tp), device_id_type=MESH)

    def start(i, carry):
        outgoing(peer(i)).start()
        return carry

    lax.fori_loop(0, n - 1, start, 0)

    def finish(i, carry):
        p = peer(i)
        outgoing(p).wait_send()
        incoming(p).wait_recv()
        return carry

    lax.fori_loop(0, n - 1, finish, 0)
    local.wait()


def dp_all_to_all(x, n, cid):
    return pl.pallas_call(
        functools.partial(a2a_kernel, n),
        out_shape=jax.ShapeDtypeStruct(x.shape, x.dtype),
        in_specs=[pl.BlockSpec(memory_space=pl.ANY)],
        out_specs=pl.BlockSpec(memory_space=pl.ANY),
        scratch_shapes=[
            pltpu.SemaphoreType.DMA((n,)),
            pltpu.SemaphoreType.DMA((n,)),
            pltpu.SemaphoreType.DMA,
        ],
        compiler_params=pltpu.CompilerParams(collective_id=cid, has_side_effects=True),
    )(x)


def expert_work(rows, grads, gate_shard, up_shard, down_shard):
    f32 = jnp.float32
    gate_value = jnp.einsum("trf,tfh->rh", rows, gate_shard, preferred_element_type=f32)
    up_value = jnp.einsum("trf,tfh->rh", rows, up_shard, preferred_element_type=f32)
    sigmoid_value = jax.nn.sigmoid(gate_value)
    silu_value = gate_value * sigmoid_value
    hidden = (silu_value * up_value).astype(jnp.bfloat16)
    hidden_grad = jnp.einsum("trf,htf->rh", grads, down_shard, preferred_element_type=f32)
    gate_grad = (
        hidden_grad * up_value * sigmoid_value * (1.0 + gate_value * (1.0 - sigmoid_value))
    ).astype(jnp.bfloat16)
    up_grad = (hidden_grad * silu_value).astype(jnp.bfloat16)
    row_part = (
        jnp.einsum("rh,tfh->trf", gate_grad, gate_shard, preferred_element_type=f32)
        + jnp.einsum("rh,tfh->trf", up_grad, up_shard, preferred_element_type=f32)
    ).astype(jnp.bfloat16)
    gate_total = jnp.einsum("trf,rh->tfh", rows, gate_grad, preferred_element_type=f32)
    up_total = jnp.einsum("trf,rh->tfh", rows, up_grad, preferred_element_type=f32)
    down_total = jnp.einsum("rh,trf->htf", hidden, grads, preferred_element_type=f32)
    return (
        row_part,
        gate_total.astype(jnp.bfloat16),
        up_total.astype(jnp.bfloat16),
        down_total.astype(jnp.bfloat16),
    )


def shards(tokens, grad_out, expert_ids, gate_probs, w_gate, w_up, w_down):
    dp_size = lax.axis_size("dp")
    tp_size = lax.axis_size("tensor")
    slices = dp_size // EXPERTS
    token_count = tokens.shape[0]
    feat = tokens.shape[1]
    pair_count = token_count * TOP
    flat_ids = expert_ids.reshape(-1)
    experts_row = jnp.arange(EXPERTS, dtype=jnp.int32)
    onehot = (flat_ids[:, None] == experts_row[None, :]).astype(jnp.int32)
    slot_index = jnp.sum((jnp.cumsum(onehot, axis=0) - onehot) * onehot, axis=1)
    positions = jnp.arange(CAP, dtype=jnp.int32)
    matches = (flat_ids[None, None, :] == experts_row[:, None, None]) & (
        slot_index[None, None, :] == positions[None, :, None]
    )
    assignment = jnp.arange(pair_count, dtype=jnp.int32)
    lookup = jnp.sum(jnp.where(matches, assignment[None, None, :], 0), axis=2)
    lookup = lookup + jnp.where(jnp.any(matches, axis=2), 0, pair_count)
    owners = jnp.arange(dp_size, dtype=jnp.int32) // slices
    send_pairs = lookup[owners]
    send_tokens = jnp.where(send_pairs < pair_count, send_pairs // TOP, token_count)
    slice_row = jnp.arange(slices, dtype=jnp.int32)
    back_index = (flat_ids[:, None] * slices + slice_row[None, :]) * CAP + slot_index[:, None]

    bf16 = jnp.bfloat16
    f32 = jnp.float32
    flat_tokens = send_tokens.reshape(-1)
    flat_pairs = send_pairs.reshape(-1)
    pick_tokens = (send_tokens[:, :, None] == jnp.arange(token_count)[None, None, :]).astype(bf16)
    pick_pairs = (send_pairs[:, :, None] == assignment[None, None, :]).astype(bf16)
    scaled = (gate_probs[:, :, None] * grad_out[:, None, :].astype(f32)).astype(bf16)
    sent_rows = jnp.einsum("pcn,nf->pcf", pick_tokens, tokens, preferred_element_type=f32)
    sent_grads = jnp.einsum(
        "pcn,nf->pcf", pick_pairs, scaled.reshape(pair_count, feat), preferred_element_type=f32
    )
    rows_count = dp_size * CAP
    got_rows = dp_all_to_all(sent_rows.astype(bf16), dp_size, 0)
    whole_rows = lax.all_gather(got_rows.reshape(rows_count, feat), "tensor", axis=0, tiled=True)
    got_grads = dp_all_to_all(sent_grads.astype(bf16), dp_size, 1)
    whole_grads = lax.all_gather(
        got_grads.reshape(rows_count, feat), "tensor", axis=0, tiled=True
    )
    got_rows = whole_rows.reshape(tp_size, rows_count, feat)
    got_grads = whole_grads.reshape(tp_size, rows_count, feat)
    hid = w_gate.shape[2]
    gate_shard = w_gate[0].reshape(tp_size, feat, hid)
    up_shard = w_up[0].reshape(tp_size, feat, hid)
    down_shard = w_down[0].reshape(hid, tp_size, feat)
    row_part, gate_total, up_total, down_total = expert_work(
        got_rows, got_grads, gate_shard, up_shard, down_shard
    )
    reduced = lax.psum_scatter(row_part, "tensor", scatter_dimension=0, tiled=True)
    gate_total = gate_total.reshape(1, tp_size * feat, hid)
    up_total = up_total.reshape(1, tp_size * feat, hid)
    down_total = down_total.reshape(1, hid, tp_size * feat)
    reduced, gate_total, up_total, down_total = lax.optimization_barrier(
        (reduced, gate_total, up_total, down_total)
    )
    returned = dp_all_to_all(reduced.reshape(dp_size, CAP, feat), dp_size, 2)
    back_flat = back_index.reshape(token_count, TOP * slices)
    rows_iota = jnp.arange(rows_count, dtype=jnp.int32).reshape(dp_size, CAP)
    gather_back = jnp.sum(
        (back_flat[:, :, None, None] == rows_iota[None, None, :, :]).astype(f32), axis=1
    ).astype(bf16)
    input_grad = jnp.einsum(
        "npc,pcf->nf", gather_back, returned, preferred_element_type=f32
    ).astype(bf16)
    return (
        input_grad,
        gate_total,
        up_total,
        down_total,
    )


def solution(mesh):
    placed = (
        P("dp", "tensor"),
        P("dp", "tensor"),
        P("dp", None),
        P("dp", None),
        P("dp", None, "tensor"),
        P("dp", None, "tensor"),
        P("dp", "tensor", None),
    )
    return jax.shard_map(
        shards,
        mesh=mesh,
        in_specs=placed,
        out_specs=(
            P("dp", "tensor"),
            P("dp", None, "tensor"),
            P("dp", None, "tensor"),
            P("dp", "tensor", None),
        ),
        check_vma=False,
    )
```

```python
import functools

import jax
import jax.numpy as jnp
from jax import lax
from jax.experimental import pallas as pl
from jax.experimental.pallas import tpu as pltpu
from jax.sharding import PartitionSpec as P

EXPERTS = 8
TOP = 2
CAP = 33
MESH = pl.DeviceIdType.MESH


def a2a_kernel(n, x_ref, y_ref, send_sem, recv_sem, local_sem):
    me = lax.axis_index("dp")
    tp = lax.axis_index("tensor")
    barrier = pltpu.get_barrier_semaphore()

    def peer(i):
        return lax.rem(me + 1 + i, n)

    def greet(i, carry):
        pl.semaphore_signal(barrier, inc=1, device_id=(peer(i), tp), device_id_type=MESH)
        return carry

    lax.fori_loop(0, n - 1, greet, 0)
    pl.semaphore_wait(barrier, n - 1)
    local = pltpu.make_async_copy(x_ref.at[me], y_ref.at[me], local_sem)
    local.start()

    def outgoing(p):
        return pltpu.make_async_remote_copy(
            src_ref=x_ref.at[p], dst_ref=y_ref.at[me], send_sem=send_sem.at[p],
            recv_sem=recv_sem.at[me], device_id=(p, tp), device_id_type=MESH)

    def incoming(p):
        return pltpu.make_async_remote_copy(
            src_ref=x_ref.at[me], dst_ref=y_ref.at[p], send_sem=send_sem.at[p],
            recv_sem=recv_sem.at[p], device_id=(p, tp), device_id_type=MESH)

    def start(i, carry):
        outgoing(peer(i)).start()
        return carry

    lax.fori_loop(0, n - 1, start, 0)

    def finish(i, carry):
        p = peer(i)
        outgoing(p).wait_send()
        incoming(p).wait_recv()
        return carry

    lax.fori_loop(0, n - 1, finish, 0)
    local.wait()


def dp_all_to_all(x, n, cid):
    return pl.pallas_call(
        functools.partial(a2a_kernel, n),
        out_shape=jax.ShapeDtypeStruct(x.shape, x.dtype),
        in_specs=[pl.BlockSpec(memory_space=pl.ANY)],
        out_specs=pl.BlockSpec(memory_space=pl.ANY),
        scratch_shapes=[
            pltpu.SemaphoreType.DMA((n,)),
            pltpu.SemaphoreType.DMA((n,)),
            pltpu.SemaphoreType.DMA,
        ],
        compiler_params=pltpu.CompilerParams(collective_id=cid, has_side_effects=True),
    )(x)


def expert_work(rows, grads, gate_shard, up_shard, down_shard):
    f32 = jnp.float32
    gate_value = jnp.einsum("trf,tfh->rh", rows, gate_shard, preferred_element_type=f32)
    up_value = jnp.einsum("trf,tfh->rh", rows, up_shard, preferred_element_type=f32)
    sigmoid_value = jax.nn.sigmoid(gate_value)
    silu_value = gate_value * sigmoid_value
    hidden = (silu_value * up_value).astype(jnp.bfloat16)
    hidden_grad = jnp.einsum("trf,htf->rh", grads, down_shard, preferred_element_type=f32)
    gate_grad = (
        hidden_grad * up_value * sigmoid_value * (1.0 + gate_value * (1.0 - sigmoid_value))
    ).astype(jnp.bfloat16)
    up_grad = (hidden_grad * silu_value).astype(jnp.bfloat16)
    row_part = (
        jnp.einsum("rh,tfh->trf", gate_grad, gate_shard, preferred_element_type=f32)
        + jnp.einsum("rh,tfh->trf", up_grad, up_shard, preferred_element_type=f32)
    ).astype(jnp.bfloat16)
    gate_total = jnp.einsum("trf,rh->tfh", rows, gate_grad, preferred_element_type=f32)
    up_total = jnp.einsum("trf,rh->tfh", rows, up_grad, preferred_element_type=f32)
    down_total = jnp.einsum("rh,trf->htf", hidden, grads, preferred_element_type=f32)
    return (
        row_part,
        gate_total.astype(jnp.bfloat16),
        up_total.astype(jnp.bfloat16),
        down_total.astype(jnp.bfloat16),
    )


def shards(tokens, grad_out, expert_ids, gate_probs, w_gate, w_up, w_down):
    dp_size = lax.axis_size("dp")
    tp_size = lax.axis_size("tensor")
    slices = dp_size // EXPERTS
    token_count = tokens.shape[0]
    feat = tokens.shape[1]
    pair_count = token_count * TOP
    flat_ids = expert_ids.reshape(-1)
    experts_row = jnp.arange(EXPERTS, dtype=jnp.int32)
    onehot = (flat_ids[:, None] == experts_row[None, :]).astype(jnp.int32)
    slot_index = jnp.sum((jnp.cumsum(onehot, axis=0) - onehot) * onehot, axis=1)
    positions = jnp.arange(CAP, dtype=jnp.int32)
    matches = (flat_ids[None, None, :] == experts_row[:, None, None]) & (
        slot_index[None, None, :] == positions[None, :, None]
    )
    assignment = jnp.arange(pair_count, dtype=jnp.int32)
    lookup = jnp.sum(jnp.where(matches, assignment[None, None, :], 0), axis=2)
    lookup = lookup + jnp.where(jnp.any(matches, axis=2), 0, pair_count)
    owners = jnp.arange(dp_size, dtype=jnp.int32) // slices
    send_pairs = lookup[owners]
    send_tokens = jnp.where(send_pairs < pair_count, send_pairs // TOP, token_count)
    slice_row = jnp.arange(slices, dtype=jnp.int32)
    back_index = (flat_ids[:, None] * slices + slice_row[None, :]) * CAP + slot_index[:, None]

    bf16 = jnp.bfloat16
    f32 = jnp.float32
    flat_tokens = send_tokens.reshape(-1)
    flat_pairs = send_pairs.reshape(-1)
    pick_tokens = (send_tokens[:, :, None] == jnp.arange(token_count)[None, None, :]).astype(bf16)
    pick_pairs = (send_pairs[:, :, None] == assignment[None, None, :]).astype(bf16)
    scaled = (gate_probs[:, :, None] * grad_out[:, None, :].astype(f32)).astype(bf16)
    sent_rows = jnp.einsum("pcn,nf->pcf", pick_tokens, tokens, preferred_element_type=f32)
    sent_grads = jnp.einsum(
        "pcn,nf->pcf", pick_pairs, scaled.reshape(pair_count, feat), preferred_element_type=f32
    )
    rows_count = dp_size * CAP
    got_rows = dp_all_to_all(sent_rows.astype(bf16), dp_size, 0)
    whole_rows = lax.all_gather(got_rows.reshape(rows_count, feat), "tensor", axis=0, tiled=True)
    got_grads = dp_all_to_all(sent_grads.astype(bf16), dp_size, 1)
    whole_grads = lax.all_gather(
        got_grads.reshape(rows_count, feat), "tensor", axis=0, tiled=True
    )
    got_rows = whole_rows.reshape(tp_size, rows_count, feat)
    got_grads = whole_grads.reshape(tp_size, rows_count, feat)
    hid = w_gate.shape[2]
    gate_shard = w_gate[0].reshape(tp_size, feat, hid)
    up_shard = w_up[0].reshape(tp_size, feat, hid)
    down_shard = w_down[0].reshape(hid, tp_size, feat)
    row_part, gate_total, up_total, down_total = expert_work(
        got_rows, got_grads, gate_shard, up_shard, down_shard
    )
    reduced = lax.psum_scatter(row_part, "tensor", scatter_dimension=0, tiled=True)
    gate_total = gate_total.reshape(1, tp_size * feat, hid)
    up_total = up_total.reshape(1, tp_size * feat, hid)
    down_total = down_total.reshape(1, hid, tp_size * feat)
    reduced, gate_total, up_total = lax.optimization_barrier((reduced, gate_total, up_total))
    returned = dp_all_to_all(reduced.reshape(dp_size, CAP, feat), dp_size, 2)
    back_flat = back_index.reshape(token_count, TOP * slices)
    rows_iota = jnp.arange(rows_count, dtype=jnp.int32).reshape(dp_size, CAP)
    gather_back = jnp.sum(
        (back_flat[:, :, None, None] == rows_iota[None, None, :, :]).astype(f32), axis=1
    ).astype(bf16)
    input_grad = jnp.einsum(
        "npc,pcf->nf", gather_back, returned, preferred_element_type=f32
    ).astype(bf16)
    return (
        input_grad,
        gate_total,
        up_total,
        down_total,
    )


def solution(mesh):
    placed = (
        P("dp", "tensor"),
        P("dp", "tensor"),
        P("dp", None),
        P("dp", None),
        P("dp", None, "tensor"),
        P("dp", None, "tensor"),
        P("dp", "tensor", None),
    )
    return jax.shard_map(
        shards,
        mesh=mesh,
        in_specs=placed,
        out_specs=(
            P("dp", "tensor"),
            P("dp", None, "tensor"),
            P("dp", None, "tensor"),
            P("dp", "tensor", None),
        ),
        check_vma=False,
    )
```

```python
import functools

import jax
import jax.numpy as jnp
from jax import lax
from jax.experimental import pallas as pl
from jax.experimental.pallas import tpu as pltpu
from jax.sharding import PartitionSpec as P

EXPERTS = 8
TOP = 2
CAP = 33
MESH = pl.DeviceIdType.MESH


def a2a_kernel(n, x_ref, y_ref, send_sem, recv_sem, local_sem):
    me = lax.axis_index("dp")
    tp = lax.axis_index("tensor")
    barrier = pltpu.get_barrier_semaphore()

    def peer(i):
        return lax.rem(me + 1 + i, n)

    def greet(i, carry):
        pl.semaphore_signal(barrier, inc=1, device_id=(peer(i), tp), device_id_type=MESH)
        return carry

    lax.fori_loop(0, n - 1, greet, 0)
    pl.semaphore_wait(barrier, n - 1)
    local = pltpu.make_async_copy(x_ref.at[me], y_ref.at[me], local_sem)
    local.start()

    def outgoing(p):
        return pltpu.make_async_remote_copy(
            src_ref=x_ref.at[p], dst_ref=y_ref.at[me], send_sem=send_sem.at[p],
            recv_sem=recv_sem.at[me], device_id=(p, tp), device_id_type=MESH)

    def incoming(p):
        return pltpu.make_async_remote_copy(
            src_ref=x_ref.at[me], dst_ref=y_ref.at[p], send_sem=send_sem.at[p],
            recv_sem=recv_sem.at[p], device_id=(p, tp), device_id_type=MESH)

    def start(i, carry):
        outgoing(peer(i)).start()
        return carry

    lax.fori_loop(0, n - 1, start, 0)

    def finish(i, carry):
        p = peer(i)
        outgoing(p).wait_send()
        incoming(p).wait_recv()
        return carry

    lax.fori_loop(0, n - 1, finish, 0)
    local.wait()


def dp_all_to_all(x, n, cid):
    return pl.pallas_call(
        functools.partial(a2a_kernel, n),
        out_shape=jax.ShapeDtypeStruct(x.shape, x.dtype),
        in_specs=[pl.BlockSpec(memory_space=pl.ANY)],
        out_specs=pl.BlockSpec(memory_space=pl.ANY),
        scratch_shapes=[
            pltpu.SemaphoreType.DMA((n,)),
            pltpu.SemaphoreType.DMA((n,)),
            pltpu.SemaphoreType.DMA,
        ],
        compiler_params=pltpu.CompilerParams(collective_id=cid, has_side_effects=True),
    )(x)


def expert_work(rows, grads, gate_shard, up_shard, down_shard):
    f32 = jnp.float32
    gate_value = jnp.einsum("trf,tfh->rh", rows, gate_shard, preferred_element_type=f32)
    up_value = jnp.einsum("trf,tfh->rh", rows, up_shard, preferred_element_type=f32)
    sigmoid_value = jax.nn.sigmoid(gate_value)
    silu_value = gate_value * sigmoid_value
    hidden = (silu_value * up_value).astype(jnp.bfloat16)
    hidden_grad = jnp.einsum("trf,htf->rh", grads, down_shard, preferred_element_type=f32)
    gate_grad = (
        hidden_grad * up_value * sigmoid_value * (1.0 + gate_value * (1.0 - sigmoid_value))
    ).astype(jnp.bfloat16)
    up_grad = (hidden_grad * silu_value).astype(jnp.bfloat16)
    row_part = (
        jnp.einsum("rh,tfh->trf", gate_grad, gate_shard, preferred_element_type=f32)
        + jnp.einsum("rh,tfh->trf", up_grad, up_shard, preferred_element_type=f32)
    ).astype(jnp.bfloat16)
    gate_total = jnp.einsum("trf,rh->tfh", rows, gate_grad, preferred_element_type=f32)
    up_total = jnp.einsum("trf,rh->tfh", rows, up_grad, preferred_element_type=f32)
    down_total = jnp.einsum("rh,trf->htf", hidden, grads, preferred_element_type=f32)
    return (
        row_part,
        gate_total.astype(jnp.bfloat16),
        up_total.astype(jnp.bfloat16),
        down_total.astype(jnp.bfloat16),
    )


def shards(tokens, grad_out, expert_ids, gate_probs, w_gate, w_up, w_down):
    dp_size = lax.axis_size("dp")
    tp_size = lax.axis_size("tensor")
    slices = dp_size // EXPERTS
    token_count = tokens.shape[0]
    feat = tokens.shape[1]
    pair_count = token_count * TOP
    flat_ids = expert_ids.reshape(-1)
    experts_row = jnp.arange(EXPERTS, dtype=jnp.int32)
    onehot = (flat_ids[:, None] == experts_row[None, :]).astype(jnp.int32)
    slot_index = jnp.sum((jnp.cumsum(onehot, axis=0) - onehot) * onehot, axis=1)
    positions = jnp.arange(CAP, dtype=jnp.int32)
    matches = (flat_ids[None, None, :] == experts_row[:, None, None]) & (
        slot_index[None, None, :] == positions[None, :, None]
    )
    slice_row = jnp.arange(slices, dtype=jnp.int32)
    back_index = (flat_ids[:, None] * slices + slice_row[None, :]) * CAP + slot_index[:, None]

    bf16 = jnp.bfloat16
    f32 = jnp.float32
    hits = matches.astype(bf16)
    pick_pairs = jnp.broadcast_to(hits[:, None], (EXPERTS, slices, CAP, pair_count))
    pick_pairs = pick_pairs.reshape(dp_size, CAP, pair_count)
    pick_tokens = jnp.sum(hits.reshape(EXPERTS, CAP, token_count, TOP), axis=3)
    pick_tokens = jnp.broadcast_to(pick_tokens[:, None], (EXPERTS, slices, CAP, token_count))
    pick_tokens = pick_tokens.reshape(dp_size, CAP, token_count)
    scaled = (gate_probs[:, :, None] * grad_out[:, None, :].astype(f32)).astype(bf16)
    sent_rows = jnp.einsum("pcn,nf->pcf", pick_tokens, tokens, preferred_element_type=f32)
    sent_grads = jnp.einsum(
        "pcn,nf->pcf", pick_pairs, scaled.reshape(pair_count, feat), preferred_element_type=f32
    )
    rows_count = dp_size * CAP
    got_rows = dp_all_to_all(sent_rows.astype(bf16), dp_size, 0)
    whole_rows = lax.all_gather(got_rows.reshape(rows_count, feat), "tensor", axis=0, tiled=True)
    got_grads = dp_all_to_all(sent_grads.astype(bf16), dp_size, 1)
    whole_grads = lax.all_gather(
        got_grads.reshape(rows_count, feat), "tensor", axis=0, tiled=True
    )
    got_rows = whole_rows.reshape(tp_size, rows_count, feat)
    got_grads = whole_grads.reshape(tp_size, rows_count, feat)
    hid = w_gate.shape[2]
    gate_shard = w_gate[0].reshape(tp_size, feat, hid)
    up_shard = w_up[0].reshape(tp_size, feat, hid)
    down_shard = w_down[0].reshape(hid, tp_size, feat)
    row_part, gate_total, up_total, down_total = expert_work(
        got_rows, got_grads, gate_shard, up_shard, down_shard
    )
    reduced = lax.psum_scatter(row_part, "tensor", scatter_dimension=0, tiled=True)
    gate_total = gate_total.reshape(1, tp_size * feat, hid)
    up_total = up_total.reshape(1, tp_size * feat, hid)
    down_total = down_total.reshape(1, hid, tp_size * feat)
    reduced, gate_total, up_total = lax.optimization_barrier((reduced, gate_total, up_total))
    returned = dp_all_to_all(reduced.reshape(dp_size, CAP, feat), dp_size, 2)
    back_flat = back_index.reshape(token_count, TOP * slices)
    rows_iota = jnp.arange(rows_count, dtype=jnp.int32).reshape(dp_size, CAP)
    gather_back = jnp.sum(
        (back_flat[:, :, None, None] == rows_iota[None, None, :, :]).astype(f32), axis=1
    ).astype(bf16)
    input_grad = jnp.einsum(
        "npc,pcf->nf", gather_back, returned, preferred_element_type=f32
    ).astype(bf16)
    return (
        input_grad,
        gate_total,
        up_total,
        down_total,
    )


def solution(mesh):
    placed = (
        P("dp", "tensor"),
        P("dp", "tensor"),
        P("dp", None),
        P("dp", None),
        P("dp", None, "tensor"),
        P("dp", None, "tensor"),
        P("dp", "tensor", None),
    )
    return jax.shard_map(
        shards,
        mesh=mesh,
        in_specs=placed,
        out_specs=(
            P("dp", "tensor"),
            P("dp", None, "tensor"),
            P("dp", None, "tensor"),
            P("dp", "tensor", None),
        ),
        check_vma=False,
    )
```

```python
import functools

import jax
import jax.numpy as jnp
from jax import lax
from jax.experimental import pallas as pl
from jax.experimental.pallas import tpu as pltpu
from jax.sharding import PartitionSpec as P

EXPERTS = 8
TOP = 2
CAP = 33
MESH = pl.DeviceIdType.MESH


def a2a_kernel(n, x_ref, y_ref, send_sem, recv_sem, local_sem):
    me = lax.axis_index("dp")
    tp = lax.axis_index("tensor")
    barrier = pltpu.get_barrier_semaphore()

    def peer(i):
        return lax.rem(me + 1 + i, n)

    def greet(i, carry):
        pl.semaphore_signal(barrier, inc=1, device_id=(peer(i), tp), device_id_type=MESH)
        return carry

    lax.fori_loop(0, n - 1, greet, 0)
    pl.semaphore_wait(barrier, n - 1)
    local = pltpu.make_async_copy(x_ref.at[me], y_ref.at[me], local_sem)
    local.start()

    def outgoing(p):
        return pltpu.make_async_remote_copy(
            src_ref=x_ref.at[p], dst_ref=y_ref.at[me], send_sem=send_sem.at[p],
            recv_sem=recv_sem.at[me], device_id=(p, tp), device_id_type=MESH)

    def incoming(p):
        return pltpu.make_async_remote_copy(
            src_ref=x_ref.at[me], dst_ref=y_ref.at[p], send_sem=send_sem.at[p],
            recv_sem=recv_sem.at[p], device_id=(p, tp), device_id_type=MESH)

    def start(i, carry):
        outgoing(peer(i)).start()
        return carry

    lax.fori_loop(0, n - 1, start, 0)

    def finish(i, carry):
        p = peer(i)
        outgoing(p).wait_send()
        incoming(p).wait_recv()
        return carry

    lax.fori_loop(0, n - 1, finish, 0)
    local.wait()


def dp_all_to_all(x, n, cid):
    return pl.pallas_call(
        functools.partial(a2a_kernel, n),
        out_shape=jax.ShapeDtypeStruct(x.shape, x.dtype),
        in_specs=[pl.BlockSpec(memory_space=pl.ANY)],
        out_specs=pl.BlockSpec(memory_space=pl.ANY),
        scratch_shapes=[
            pltpu.SemaphoreType.DMA((n,)),
            pltpu.SemaphoreType.DMA((n,)),
            pltpu.SemaphoreType.DMA,
        ],
        compiler_params=pltpu.CompilerParams(collective_id=cid, has_side_effects=True),
    )(x)


def expert_work(rows, grads, gate_shard, up_shard, down_shard):
    f32 = jnp.float32
    gate_value = jnp.einsum("trf,tfh->rh", rows, gate_shard, preferred_element_type=f32)
    up_value = jnp.einsum("trf,tfh->rh", rows, up_shard, preferred_element_type=f32)
    sigmoid_value = jax.nn.sigmoid(gate_value)
    silu_value = gate_value * sigmoid_value
    hidden = (silu_value * up_value).astype(jnp.bfloat16)
    hidden_grad = jnp.einsum("trf,htf->rh", grads, down_shard, preferred_element_type=f32)
    gate_grad = (
        hidden_grad * up_value * sigmoid_value * (1.0 + gate_value * (1.0 - sigmoid_value))
    ).astype(jnp.bfloat16)
    up_grad = (hidden_grad * silu_value).astype(jnp.bfloat16)
    row_part = (
        jnp.einsum("rh,tfh->trf", gate_grad, gate_shard, preferred_element_type=f32)
        + jnp.einsum("rh,tfh->trf", up_grad, up_shard, preferred_element_type=f32)
    ).astype(jnp.bfloat16)
    gate_total = jnp.einsum("trf,rh->tfh", rows, gate_grad, preferred_element_type=f32)
    up_total = jnp.einsum("trf,rh->tfh", rows, up_grad, preferred_element_type=f32)
    down_total = jnp.einsum("rh,trf->htf", hidden, grads, preferred_element_type=f32)
    return (
        row_part,
        gate_total.astype(jnp.bfloat16),
        up_total.astype(jnp.bfloat16),
        down_total.astype(jnp.bfloat16),
    )


def shards(tokens, grad_out, expert_ids, gate_probs, w_gate, w_up, w_down):
    dp_size = lax.axis_size("dp")
    tp_size = lax.axis_size("tensor")
    slices = dp_size // EXPERTS
    token_count = tokens.shape[0]
    feat = tokens.shape[1]
    pair_count = token_count * TOP
    flat_ids = expert_ids.reshape(-1)
    experts_row = jnp.arange(EXPERTS, dtype=jnp.int32)
    onehot = (flat_ids[:, None] == experts_row[None, :]).astype(jnp.int32)
    slot_index = jnp.sum((jnp.cumsum(onehot, axis=0) - onehot) * onehot, axis=1)
    positions = jnp.arange(CAP, dtype=jnp.int32)
    matches = (flat_ids[None, None, :] == experts_row[:, None, None]) & (
        slot_index[None, None, :] == positions[None, :, None]
    )

    bf16 = jnp.bfloat16
    f32 = jnp.float32
    hits = matches.astype(bf16)
    pick_pairs = jnp.broadcast_to(hits[:, None], (EXPERTS, slices, CAP, pair_count))
    pick_pairs = pick_pairs.reshape(dp_size, CAP, pair_count)
    pick_tokens = jnp.sum(hits.reshape(EXPERTS, CAP, token_count, TOP), axis=3)
    pick_tokens = jnp.broadcast_to(pick_tokens[:, None], (EXPERTS, slices, CAP, token_count))
    pick_tokens = pick_tokens.reshape(dp_size, CAP, token_count)
    scaled = (gate_probs[:, :, None] * grad_out[:, None, :].astype(f32)).astype(bf16)
    sent_rows = jnp.einsum("pcn,nf->pcf", pick_tokens, tokens, preferred_element_type=f32)
    sent_grads = jnp.einsum(
        "pcn,nf->pcf", pick_pairs, scaled.reshape(pair_count, feat), preferred_element_type=f32
    )
    rows_count = dp_size * CAP
    got_rows = dp_all_to_all(sent_rows.astype(bf16), dp_size, 0)
    whole_rows = lax.all_gather(got_rows.reshape(rows_count, feat), "tensor", axis=0, tiled=True)
    got_grads = dp_all_to_all(sent_grads.astype(bf16), dp_size, 1)
    whole_grads = lax.all_gather(
        got_grads.reshape(rows_count, feat), "tensor", axis=0, tiled=True
    )
    got_rows = whole_rows.reshape(tp_size, rows_count, feat)
    got_grads = whole_grads.reshape(tp_size, rows_count, feat)
    hid = w_gate.shape[2]
    gate_shard = w_gate[0].reshape(tp_size, feat, hid)
    up_shard = w_up[0].reshape(tp_size, feat, hid)
    down_shard = w_down[0].reshape(hid, tp_size, feat)
    row_part, gate_total, up_total, down_total = expert_work(
        got_rows, got_grads, gate_shard, up_shard, down_shard
    )
    reduced = lax.psum_scatter(row_part, "tensor", scatter_dimension=0, tiled=True)
    gate_total = gate_total.reshape(1, tp_size * feat, hid)
    up_total = up_total.reshape(1, tp_size * feat, hid)
    down_total = down_total.reshape(1, hid, tp_size * feat)
    reduced, gate_total, up_total = lax.optimization_barrier((reduced, gate_total, up_total))
    returned = dp_all_to_all(reduced.reshape(dp_size, CAP, feat), dp_size, 2)
    input_grad = jnp.einsum(
        "pcn,pcf->nf", pick_tokens, returned, preferred_element_type=f32
    ).astype(bf16)
    return (
        input_grad,
        gate_total,
        up_total,
        down_total,
    )


def solution(mesh):
    placed = (
        P("dp", "tensor"),
        P("dp", "tensor"),
        P("dp", None),
        P("dp", None),
        P("dp", None, "tensor"),
        P("dp", None, "tensor"),
        P("dp", "tensor", None),
    )
    return jax.shard_map(
        shards,
        mesh=mesh,
        in_specs=placed,
        out_specs=(
            P("dp", "tensor"),
            P("dp", None, "tensor"),
            P("dp", None, "tensor"),
            P("dp", "tensor", None),
        ),
        check_vma=False,
    )
```

```python
import functools

import jax
import jax.numpy as jnp
from jax import lax
from jax.experimental import pallas as pl
from jax.experimental.pallas import tpu as pltpu
from jax.sharding import PartitionSpec as P

EXPERTS = 8
TOP = 2
CAP = 33
MESH = pl.DeviceIdType.MESH


def a2a_kernel(n, x_ref, y_ref, send_sem, recv_sem, local_sem):
    me = lax.axis_index("dp")
    tp = lax.axis_index("tensor")
    barrier = pltpu.get_barrier_semaphore()

    def peer(i):
        return lax.rem(me + 1 + i, n)

    def greet(i, carry):
        pl.semaphore_signal(barrier, inc=1, device_id=(peer(i), tp), device_id_type=MESH)
        return carry

    lax.fori_loop(0, n - 1, greet, 0)
    pl.semaphore_wait(barrier, n - 1)
    local = pltpu.make_async_copy(x_ref.at[me], y_ref.at[me], local_sem)
    local.start()

    def outgoing(p):
        return pltpu.make_async_remote_copy(
            src_ref=x_ref.at[p], dst_ref=y_ref.at[me], send_sem=send_sem.at[p],
            recv_sem=recv_sem.at[me], device_id=(p, tp), device_id_type=MESH)

    def incoming(p):
        return pltpu.make_async_remote_copy(
            src_ref=x_ref.at[me], dst_ref=y_ref.at[p], send_sem=send_sem.at[p],
            recv_sem=recv_sem.at[p], device_id=(p, tp), device_id_type=MESH)

    def start(i, carry):
        outgoing(peer(i)).start()
        return carry

    lax.fori_loop(0, n - 1, start, 0)

    def finish(i, carry):
        p = peer(i)
        outgoing(p).wait_send()
        incoming(p).wait_recv()
        return carry

    lax.fori_loop(0, n - 1, finish, 0)
    local.wait()


def dp_all_to_all(x, n, cid):
    return pl.pallas_call(
        functools.partial(a2a_kernel, n),
        out_shape=jax.ShapeDtypeStruct(x.shape, x.dtype),
        in_specs=[pl.BlockSpec(memory_space=pl.ANY)],
        out_specs=pl.BlockSpec(memory_space=pl.ANY),
        scratch_shapes=[
            pltpu.SemaphoreType.DMA((n,)),
            pltpu.SemaphoreType.DMA((n,)),
            pltpu.SemaphoreType.DMA,
        ],
        compiler_params=pltpu.CompilerParams(collective_id=cid, has_side_effects=True),
    )(x)


def expert_work(rows, grads, gate_shard, up_shard, down_shard):
    f32 = jnp.float32
    gate_value = jnp.einsum("trf,tfh->rh", rows, gate_shard, preferred_element_type=f32)
    up_value = jnp.einsum("trf,tfh->rh", rows, up_shard, preferred_element_type=f32)
    sigmoid_value = jax.nn.sigmoid(gate_value)
    silu_value = gate_value * sigmoid_value
    hidden = (silu_value * up_value).astype(jnp.bfloat16)
    hidden_grad = jnp.einsum("trf,htf->rh", grads, down_shard, preferred_element_type=f32)
    gate_grad = (
        hidden_grad * up_value * sigmoid_value * (1.0 + gate_value * (1.0 - sigmoid_value))
    ).astype(jnp.bfloat16)
    up_grad = (hidden_grad * silu_value).astype(jnp.bfloat16)
    row_part = (
        jnp.einsum("rh,tfh->trf", gate_grad, gate_shard, preferred_element_type=f32)
        + jnp.einsum("rh,tfh->trf", up_grad, up_shard, preferred_element_type=f32)
    ).astype(jnp.bfloat16)
    gate_total = jnp.einsum("trf,rh->tfh", rows, gate_grad, preferred_element_type=f32)
    up_total = jnp.einsum("trf,rh->tfh", rows, up_grad, preferred_element_type=f32)
    down_total = jnp.einsum("rh,trf->htf", hidden, grads, preferred_element_type=f32)
    return (
        row_part,
        gate_total.astype(jnp.bfloat16),
        up_total.astype(jnp.bfloat16),
        down_total.astype(jnp.bfloat16),
    )


def shards(tokens, grad_out, expert_ids, gate_probs, w_gate, w_up, w_down):
    dp_size = lax.axis_size("dp")
    tp_size = lax.axis_size("tensor")
    slices = dp_size // EXPERTS
    token_count = tokens.shape[0]
    feat = tokens.shape[1]
    pair_count = token_count * TOP
    flat_ids = expert_ids.T.reshape(-1)
    experts_row = jnp.arange(EXPERTS, dtype=jnp.int32)
    onehot = (flat_ids[:, None] == experts_row[None, :]).astype(jnp.int32)
    slot_index = jnp.sum((jnp.cumsum(onehot, axis=0) - onehot) * onehot, axis=1)
    positions = jnp.arange(CAP, dtype=jnp.int32)
    matches = (flat_ids[None, None, :] == experts_row[:, None, None]) & (
        slot_index[None, None, :] == positions[None, :, None]
    )

    bf16 = jnp.bfloat16
    f32 = jnp.float32
    hits = matches.astype(bf16)
    pick_pairs = jnp.broadcast_to(hits[:, None], (EXPERTS, slices, CAP, pair_count))
    pick_pairs = pick_pairs.reshape(dp_size, CAP, pair_count)
    pick_tokens = jnp.sum(hits.reshape(EXPERTS, CAP, TOP, token_count), axis=2)
    pick_tokens = jnp.broadcast_to(pick_tokens[:, None], (EXPERTS, slices, CAP, token_count))
    pick_tokens = pick_tokens.reshape(dp_size, CAP, token_count)
    scaled = (gate_probs.T[:, :, None] * grad_out[None, :, :].astype(f32)).astype(bf16)
    sent_rows = jnp.einsum("pcn,nf->pcf", pick_tokens, tokens, preferred_element_type=f32)
    sent_grads = jnp.einsum(
        "pcn,nf->pcf", pick_pairs, scaled.reshape(pair_count, feat), preferred_element_type=f32
    )
    rows_count = dp_size * CAP
    got_rows = dp_all_to_all(sent_rows.astype(bf16), dp_size, 0)
    whole_rows = lax.all_gather(got_rows.reshape(rows_count, feat), "tensor", axis=0, tiled=True)
    got_grads = dp_all_to_all(sent_grads.astype(bf16), dp_size, 1)
    whole_grads = lax.all_gather(
        got_grads.reshape(rows_count, feat), "tensor", axis=0, tiled=True
    )
    got_rows = whole_rows.reshape(tp_size, rows_count, feat)
    got_grads = whole_grads.reshape(tp_size, rows_count, feat)
    hid = w_gate.shape[2]
    gate_shard = w_gate[0].reshape(tp_size, feat, hid)
    up_shard = w_up[0].reshape(tp_size, feat, hid)
    down_shard = w_down[0].reshape(hid, tp_size, feat)
    row_part, gate_total, up_total, down_total = expert_work(
        got_rows, got_grads, gate_shard, up_shard, down_shard
    )
    reduced = lax.psum_scatter(row_part, "tensor", scatter_dimension=0, tiled=True)
    gate_total = gate_total.reshape(1, tp_size * feat, hid)
    up_total = up_total.reshape(1, tp_size * feat, hid)
    down_total = down_total.reshape(1, hid, tp_size * feat)
    reduced, gate_total, up_total = lax.optimization_barrier((reduced, gate_total, up_total))
    returned = dp_all_to_all(reduced.reshape(dp_size, CAP, feat), dp_size, 2)
    input_grad = jnp.einsum(
        "pcn,pcf->nf", pick_tokens, returned, preferred_element_type=f32
    ).astype(bf16)
    return (
        input_grad,
        gate_total,
        up_total,
        down_total,
    )


def solution(mesh):
    placed = (
        P("dp", "tensor"),
        P("dp", "tensor"),
        P("dp", None),
        P("dp", None),
        P("dp", None, "tensor"),
        P("dp", None, "tensor"),
        P("dp", "tensor", None),
    )
    return jax.shard_map(
        shards,
        mesh=mesh,
        in_specs=placed,
        out_specs=(
            P("dp", "tensor"),
            P("dp", None, "tensor"),
            P("dp", None, "tensor"),
            P("dp", "tensor", None),
        ),
        check_vma=False,
    )
```
